32 devices in a mesh: lon: 2 (over x), lat: 4 (over z), lev: 4 (over y, core).
Axes of the slice: x: 2, y: 2, z: 4, core: 2. Of those that a mesh axis runs over, the one named last changes fastest.
Arguments:
- adjoint_in: float32 [8, 16, 16, 512], P(None, 'lev', 'lat', 'lon'), may hold values from -6 to 6
- courant_lon: float32 [16, 16, 512], P('lev', 'lat', 'lon'), may hold values from 0.05 to 0.45
- courant_lat: float32 [16, 16, 512], P('lev', 'lat', 'lon'), may hold values from 0.05 to 0.25
- horiz_diff: float32 [8], replicated, may hold values from 0.01 to 0.06
- vert_diff: float32 [16], replicated, may hold values from 0.01 to 0.1
- innovations: bfloat16 [512, 8, 16, 128], P(('lon', 'lat'), None, 'lev'), may hold values from -6 to 6
- obs_operator: bfloat16 [512, 128, 256], P(('lon', 'lat')), may hold values from -0.5 to 0.5
- owner_tile: int32 [512, 1], P(('lon', 'lat')), may hold values from 0 to 1; in each aligned block of 64 rows (0 to 63, 64 to 127, ...) at most 64 rows name the same one
- block_row: int32 [512], P(('lon', 'lat')), may hold values from 0 to 3
- obs_count: int32 [512], P(('lon', 'lat')), may hold values from 1 to 128
Outputs:
- adjoint_out: float32 [8, 16, 16, 512], P(None, 'lev', 'lat', 'lon')
The draws below stay inside these ranges and needn't reach their ends.
Inputs may be any that keep to these rules, and one draw needn't show every extreme that they name: `owner_tile`: among the 64 blocks of one device at most 64 name the same longitude tile; in some device exactly 64 do.
All inputs are finite; a program needn't handle non-finite values.
Results may differ from the reference program's by a relative error of at most 0.002.
The reference program's roundings to bfloat16 on the way (of `observed` and `products`) count: a program that leaves them out, or rounds other values in their place, can miss the bound.
Values may be sent and summed in bfloat16 or wider, within the bound.
No kernel may reach another device: no remote copies, remote signals or barrier semaphores. Data moves between devices by JAX's collectives and lax.ppermute only.
A program may use at most 64 MiB of HBM per device.

```python
import math
import jax
import jax.numpy as jnp
import numpy as np
from jax import lax

F = 8
OBS = 128
CLON = 256
STEPS = 3
CLAT = 4
BLK_DEV = 64
LEVELS = 16
NLAT = 16
NLON = 512
NBLK = 512
CAP = 64
N_LON = 2
N_LAT = 4


def set_ends(entries, rng, low, largest):
    spot = [jax.random.randint(jax.random.fold_in(rng, axis), (), 0, length) for axis, length in enumerate(entries.shape)]
    widest = entries.shape.index(max(entries.shape))
    neighbour = spot[:widest] + [(spot[widest] + 1) % entries.shape[widest]] + spot[widest + 1:]
    return entries.at[tuple(spot)].set(low).at[tuple(neighbour)].set(largest)


def shard_levels(stream_key, extent, shards, least, largest):
    def one(position, parts):
        heights = jax.random.uniform(jax.random.fold_in(jax.random.fold_in(stream_key, 6), position), (parts,), jnp.float32, least / len(shards), largest / len(shards))
        return jnp.repeat(jnp.exp(heights), extent[position] // parts).reshape((-1,) + (1,) * (len(extent) - position - 1))

    loudness = one(*shards[0])
    for cut in shards[1:]:
        loudness = loudness * one(*cut)
    return loudness


def routed_block(stream_key, own, number, rows, count, top, reach, lean):
    order = jax.random.permutation(stream_key, count)
    heavy_load, common = portions_of(count, rows * top, reach, lean, True), portions_of(count, rows * top, reach, lean, False)
    places = jnp.arange(count)

    def named(lengths, offset_by):
        used = int((lengths > 0).sum())
        fixed = max(1, used // 4)
        passed = fixed + (places - fixed + offset_by * (used - fixed)) % max(1, count - fixed)
        return jnp.zeros((count,), jnp.int32).at[order[jnp.where(places < fixed, places, passed)]].set(jnp.asarray(lengths, jnp.int32))

    lengths = jnp.where(number % 4 == 0, named(heavy_load, number // 4), named(common, number - number // 4 - 1))
    mixed = jax.random.permutation(jax.random.fold_in(own, 3), count)
    donor, sink = mixed[0:count // 2 * 2:2], mixed[1:count // 2 * 2:2]
    margin = jnp.minimum(lengths[donor] - 1, reach - lengths[sink]) // 2
    margin = jnp.where((donor == order[0]) | (sink == order[0]) | (lengths[sink] == 0), 0, jnp.maximum(margin, 0))
    passed = jax.random.randint(jax.random.fold_in(own, 4), (count // 2,), 0, 1 << 20) % (margin + 1)
    lengths = lengths.at[donor].add(-passed).at[sink].add(passed)
    labels = jnp.searchsorted(jnp.cumsum(lengths), jnp.arange(rows * top), side="right").astype(jnp.int32)
    grid = labels.reshape(top, rows).T
    grid = grid[jax.random.permutation(jax.random.fold_in(own, 1), rows)]
    offset_by = jax.random.randint(jax.random.fold_in(own, 2), (rows, 1), 0, top)
    return jnp.take_along_axis(grid, (jnp.arange(top)[None, :] + offset_by) % top, axis=1)


def portions_of(number_of, total, bound, lean, full):
    portions = [(1 << 20) // math.isqrt(rank ** lean) + 1 for rank in range(1, number_of + 1)]
    largest = bound if full else min(bound, max(-(-total // number_of), total * portions[0] // sum(portions)))
    least = 1 if total - largest >= number_of - 1 else 0
    given, spare = [largest] + [least] * (number_of - 1), total - largest - least * (number_of - 1)
    while spare > 0:
        free = [i for i in range(1, number_of) if given[i] < largest] or [i for i in range(1, number_of) if given[i] < bound]
        pool, budget = sum([portions[i] for i in free]), spare
        for i in free:
            addition = min(bound - given[i], max(1, budget * portions[i] // pool), spare)
            given[i] = given[i] + addition
            spare = spare - addition
    return np.array(given)


def noise(key, shape, spread, limit, split=(), held_as=jnp.bfloat16):
    values = jax.random.normal(key, shape, jnp.float32) * spread
    if len(split) > 0:
        values = shard_levels(key, shape, split, -0.22, 0.18) * values
    return jnp.clip(values, min=-limit, max=limit).astype(held_as)


def setup_inputs(seed: int = 0) -> dict:
    arg_keys = jax.random.split(jax.random.key(seed), 11)
    adjoint_in = noise(arg_keys[0], (F, LEVELS, NLAT, NLON), 1.0, 6.0, ((1, 4), (2, 4), (3, 2)), jnp.float32)
    courant_lon = jnp.clip(jnp.exp(math.log(0.45) - 2.1972245 * jax.random.uniform(arg_keys[1], (LEVELS, NLAT, NLON), jnp.float32) ** shard_levels(arg_keys[1], (LEVELS, NLAT, NLON), ((0, 4), (1, 4), (2, 2)), -0.2, 0.2)), 0.05, 0.45)
    courant_lat = jnp.clip(jnp.exp(math.log(0.25) - 1.609438 * jax.random.uniform(arg_keys[2], (LEVELS, NLAT, NLON), jnp.float32) ** shard_levels(arg_keys[2], (LEVELS, NLAT, NLON), ((0, 4), (1, 4), (2, 2)), -0.2, 0.2)), 0.05, 0.25)
    horiz_diff = jnp.clip(jnp.exp(jax.random.uniform(arg_keys[3], (F,), jnp.float32, math.log(0.01), math.log(0.06))), 0.01, 0.06)
    vert_diff = jnp.clip(jnp.exp(jax.random.uniform(arg_keys[4], (LEVELS,), jnp.float32, math.log(0.01), math.log(0.1))), 0.01, 0.1)
    innovations = noise(arg_keys[5], (NBLK, F, LEVELS, OBS), 1.0, 6.0, ((0, 8), (2, 4)))
    obs_operator = noise(arg_keys[6], (NBLK, OBS, CLON), OBS ** -0.5, 0.5, ((0, 8),))
    owner_tile_keys = jax.random.split(jax.random.fold_in(arg_keys[7], 1), NBLK // BLK_DEV)
    owner_tile_turns = jax.random.permutation(jax.random.fold_in(arg_keys[7], 3), NBLK // BLK_DEV)
    owner_tile = jax.vmap(lambda own, number: routed_block(jax.random.fold_in(arg_keys[7], 2), own, number, BLK_DEV, N_LON, 1, CAP, 2))(owner_tile_keys, owner_tile_turns).reshape((NBLK, 1))
    block_row = set_ends(jax.random.randint(arg_keys[8], (NBLK,), 0, CLAT), jax.random.fold_in(arg_keys[8], 1), 0, CLAT - 1).astype(jnp.int32)
    obs_count = set_ends(jax.random.randint(arg_keys[9], (NBLK,), 1, OBS + 1), jax.random.fold_in(arg_keys[9], 1), 1, OBS).astype(jnp.int32)
    return dict(adjoint_in=adjoint_in, courant_lon=courant_lon, courant_lat=courant_lat, horiz_diff=horiz_diff, vert_diff=vert_diff, innovations=innovations, obs_operator=obs_operator, owner_tile=owner_tile, block_row=block_row, obs_count=obs_count)


def adjoint_step(adjoint, courant_lon, courant_lat, horiz_diff, coef_up, coef_down):
    east_flux = courant_lon[None] * adjoint
    north_flux = courant_lat[None] * adjoint
    east_side = jnp.roll(adjoint, -1, axis=3)
    west_side = jnp.roll(adjoint, 1, axis=3)
    east_moved = jnp.roll(east_flux, -1, axis=3)
    zero_row = jnp.zeros_like(adjoint[:, :, :1])
    north_side = jnp.concatenate([adjoint[:, :, 1:], zero_row], axis=2)
    south_side = jnp.concatenate([zero_row, adjoint[:, :, :-1]], axis=2)
    north_moved = jnp.concatenate([north_flux[:, :, 1:], zero_row], axis=2)
    zero_level = jnp.zeros_like(adjoint[:, :1])
    level_above = jnp.concatenate([adjoint[:, 1:], zero_level], axis=1)
    level_below = jnp.concatenate([zero_level, adjoint[:, :-1]], axis=1)
    diff_gain = horiz_diff[:, None, None, None]
    result = adjoint - east_flux - north_flux + east_moved + north_moved
    result = result + diff_gain * (east_side + west_side + north_side + south_side - 4.0 * adjoint)
    result = result + coef_up[None, :, None, None] * (level_above - adjoint)
    result = result + coef_down[None, :, None, None] * (level_below - adjoint)
    return result


def reference(adjoint_in, courant_lon, courant_lat, horiz_diff, vert_diff, innovations, obs_operator, owner_tile, block_row, obs_count):
    groups = NBLK // BLK_DEV
    level_ids = jnp.arange(LEVELS, dtype=jnp.int32)
    coef_up = jnp.where(level_ids < LEVELS - 1, vert_diff, jnp.zeros_like(vert_diff))
    coef_down = jnp.concatenate([jnp.zeros((1,), vert_diff.dtype), vert_diff[:-1]])
    adjoint = adjoint_in
    for sub_step in range(STEPS):
        adjoint = adjoint_step(adjoint, courant_lon, courant_lat, horiz_diff, coef_up, coef_down)

    group_innov = innovations.reshape(groups, BLK_DEV, F, LEVELS, OBS)
    group_ops = obs_operator.reshape(groups, BLK_DEV, OBS, CLON)
    group_tiles = owner_tile[:, 0].reshape(groups, BLK_DEV)
    group_rows = block_row.reshape(groups, BLK_DEV)
    group_counts = obs_count.reshape(groups, BLK_DEV)
    group_ids = jnp.arange(groups, dtype=jnp.int32)

    def add_group(column_sum, group_items):
        group_id, block_innov, block_ops, lon_tiles, lat_rows, counts_here = group_items
        observed = jnp.arange(OBS, dtype=jnp.int32)[None, :] < counts_here[:, None]
        masked = jnp.where(observed[:, None, None, :], block_innov, jnp.zeros_like(block_innov))
        products = jnp.einsum("bfko,boc->fkbc", masked.astype(jnp.float32), block_ops.astype(jnp.float32)).astype(jnp.bfloat16)
        products = lax.optimization_barrier(products).astype(jnp.float32)
        global_rows = ((group_id % N_LAT) * CLAT + lat_rows).astype(jnp.int32)
        column_sum = column_sum.at[:, :, global_rows, lon_tiles.astype(jnp.int32), :].add(products)
        return column_sum, None

    start_sum = jnp.zeros((F, LEVELS, NLAT, N_LON, CLON), jnp.float32)
    column_sum, unused = lax.scan(add_group, start_sum, (group_ids, group_innov, group_ops, group_tiles, group_rows, group_counts))
    obs_gradient = column_sum.reshape(F, LEVELS, NLAT, NLON)
    return adjoint + obs_gradient
```

```python
import jax
import jax.numpy as jnp
from jax import lax
from jax.sharding import PartitionSpec as P

STEPS = 3


def extended_2(block, sides, width, periodic):
    for axis, dim in sides:
        count = lax.axis_size(axis)
        forward = [(i, i + 1) for i in range(count - 1)]
        if periodic:
            forward.append((count - 1, 0))
        backward = [(target, source) for source, target in forward]
        low = lax.ppermute(
            lax.slice_in_dim(block, block.shape[dim] - width, None, axis=dim), axis, forward
        )
        high = lax.ppermute(lax.slice_in_dim(block, 0, width, axis=dim), axis, backward)
        block = jnp.concatenate([low, block, high], axis=dim)
    return block


def widen(field, rim_width):
    beside_all = extended_2(field, (("lon", 3),), rim_width, True)
    return extended_2(beside_all, (("lat", 2), ("lev", 1)), rim_width, False)


def sweep(
    extended,
    wind_pair,
    horiz_diff,
    vert_diff,
    rim_width,
    lev_first,
    lat_first,
    level_total,
    lat_total,
):
    out_rim = rim_width - 1
    lev_glob = lev_first - out_rim + jnp.arange(extended.shape[1] - 2, dtype=jnp.int32)
    lat_glob = lat_first - out_rim + jnp.arange(extended.shape[2] - 2, dtype=jnp.int32)
    level_ids = jnp.arange(level_total, dtype=jnp.int32)
    coef_up = jnp.sum(
        jnp.where(
            (lev_glob[:, None] == level_ids[None, :]) & (level_ids[None, :] < level_total - 1),
            vert_diff[None, :],
            0.0,
        ),
        axis=1,
    )
    coef_down = jnp.sum(
        jnp.where(lev_glob[:, None] - 1 == level_ids[None, :], vert_diff[None, :], 0.0), axis=1
    )
    inside = (
        ((lev_glob >= 0) & (lev_glob < level_total))[:, None]
        & ((lat_glob >= 0) & (lat_glob < lat_total))[None, :]
    ).astype(jnp.float32)
    east_flux = wind_pair[0][None] * extended
    north_flux = wind_pair[1][None] * extended
    centre = extended[:, 1:-1, 1:-1, 1:-1]
    result = centre - east_flux[:, 1:-1, 1:-1, 1:-1] - north_flux[:, 1:-1, 1:-1, 1:-1]
    result = result + east_flux[:, 1:-1, 1:-1, 2:] + north_flux[:, 1:-1, 2:, 1:-1]
    spread = (
        extended[:, 1:-1, 1:-1, 2:]
        + extended[:, 1:-1, 1:-1, :-2]
        + extended[:, 1:-1, 2:, 1:-1]
        + extended[:, 1:-1, :-2, 1:-1]
        - 4.0 * centre
    )
    result = result + horiz_diff[:, None, None, None] * spread
    result = result + coef_up[None, :, None, None] * (extended[:, 2:, 1:-1, 1:-1] - centre)
    result = result + coef_down[None, :, None, None] * (extended[:, :-2, 1:-1, 1:-1] - centre)
    return result * inside[None, :, :, None]


def on_device(
    adjoint_in,
    courant_lon,
    courant_lat,
    horiz_diff,
    vert_diff,
    innovations,
    obs_operator,
    owner_tile,
    block_row,
    obs_count,
):
    num_fields = adjoint_in.shape[0]
    lev_cells = adjoint_in.shape[1]
    lat_cells = adjoint_in.shape[2]
    lon_cells = adjoint_in.shape[3]
    num_blocks = innovations.shape[0]
    obs_rows = innovations.shape[3]
    level_total = lev_cells * lax.axis_size("lev")
    lat_total = lat_cells * lax.axis_size("lat")
    lev_first = lax.axis_index("lev") * lev_cells
    lat_first = lax.axis_index("lat") * lat_cells
    observed = jnp.arange(obs_rows, dtype=jnp.int32)[None, :] < obs_count[:, None]
    masked = jnp.where(observed[:, None, None, :], innovations, jnp.zeros((), jnp.bfloat16))
    masked = masked.reshape(num_blocks, num_fields * lev_cells, obs_rows)
    products = jnp.einsum(
        "bvo,boc->bvc", masked, obs_operator, preferred_element_type=jnp.float32
    ).astype(jnp.bfloat16)
    flattened = products.reshape(num_blocks, num_fields * lev_cells * lon_cells)
    dest_tile = owner_tile[:, 0]
    target = dest_tile * lat_cells + block_row
    picks = (
        jnp.arange(lax.axis_size("lon") * lat_cells, dtype=jnp.int32)[:, None] == target[None, :]
    ).astype(jnp.bfloat16)
    partial_sums = jnp.dot(picks, flattened, preferred_element_type=jnp.float32)
    if lax.axis_size("lon") == 2:
        my_lon = lax.axis_index("lon")
        mine = lax.dynamic_slice_in_dim(partial_sums, my_lon * lat_cells, lat_cells, 0)
        other = lax.dynamic_slice_in_dim(partial_sums, (1 - my_lon) * lat_cells, lat_cells, 0)
        obs_sum = mine + lax.ppermute(other, "lon", [(0, 1), (1, 0)])
    else:
        obs_sum = lax.psum_scatter(partial_sums, "lon", scatter_dimension=0, tiled=True)
    obs_gradient = obs_sum.reshape(lat_cells, num_fields, lev_cells, lon_cells).transpose(
        1, 2, 0, 3
    )
    wind_pair = jnp.stack([courant_lon, courant_lat])
    joined = jnp.concatenate([adjoint_in, wind_pair], axis=0)
    widened = widen(joined, STEPS)
    adjoint = widened[:num_fields]
    for sub_step in range(STEPS):
        rim_width = STEPS - sub_step
        wind_wide = widened[
            num_fields:,
            sub_step : sub_step + lev_cells + 2 * rim_width,
            sub_step : sub_step + lat_cells + 2 * rim_width,
            sub_step : sub_step + lon_cells + 2 * rim_width,
        ]
        adjoint = sweep(
            adjoint,
            wind_wide,
            horiz_diff,
            vert_diff,
            rim_width,
            lev_first,
            lat_first,
            level_total,
            lat_total,
        )
    return adjoint + obs_gradient


def solution(mesh):
    in_specs = (
        P(None, "lev", "lat", "lon"),
        P("lev", "lat", "lon"),
        P("lev", "lat", "lon"),
        P(),
        P(),
        P(("lon", "lat"), None, "lev", None),
        P(("lon", "lat"), None, None),
        P(("lon", "lat"), None),
        P(("lon", "lat")),
        P(("lon", "lat")),
    )
    out_specs = P(None, "lev", "lat", "lon")
    return jax.shard_map(
        on_device, mesh=mesh, in_specs=in_specs, out_specs=out_specs, check_vma=False
    )
```

```python
import functools

import jax
import jax.numpy as jnp
from jax import lax
from jax.experimental import pallas as pl
from jax.experimental.pallas import tpu as pltpu
from jax.sharding import PartitionSpec as P

STEPS = 3
LANES = 128
GROUP = 16
PER_TILE = LANES // GROUP
VMEM = pl.BlockSpec(memory_space=pltpu.VMEM)
SMEM = pl.BlockSpec(memory_space=pltpu.SMEM)
ANY = pl.BlockSpec(memory_space=pl.ANY)
HBM = pl.BlockSpec(memory_space=pltpu.HBM)


PARAMS = pltpu.CompilerParams(vmem_limit_bytes=12 << 20)


def cost(flops, nbytes):
    return pl.CostEstimate(flops=flops, bytes_accessed=nbytes, transcendentals=0)


def pair_up(count, phase, others, major):
    pairs = []
    for i in range(count):
        mate = i + 1 if i % 2 == phase else i - 1
        for j in range(others):
            to = (mate, j) if 0 <= mate < count else (i, j ^ 1)
            if to[1] < others:
                ends = [p * others + q if major else q * count + p for p, q in ((i, j), to)]
                pairs.append(tuple(ends))
    return pairs


def lev_rows(lat_cells):
    return [(d, -(STEPS - d), lat_cells + 2 * (STEPS - d)) for d in range(1, STEPS + 1)]


def load_kernel(adj, wind_u, wind_w, *refs):
    small, (own, to_a, to_b), small_out, sem = refs[:3], refs[3:6], refs[6:9], refs[9]
    fields, levs, lats = adj.shape[:3]
    copies = [
        pltpu.make_async_copy(adj.at[f], own.at[:, 0:lats, f, :], sem.at[f]) for f in range(fields)
    ]
    copies.append(pltpu.make_async_copy(wind_u, own.at[:, lats, 0:lats, :], sem.at[fields]))
    copies.append(
        pltpu.make_async_copy(wind_w, own.at[:, lats, lats : 2 * lats, :], sem.at[fields + 1])
    )
    for n, (source, target) in enumerate(zip(small, small_out)):
        copies.append(pltpu.make_async_copy(source, target, sem.at[fields + 2 + n]))
    for copy in copies:
        copy.start()
    for copy in copies:
        copy.wait()
    odd = lax.rem(lax.axis_index("lat"), 2)
    for out, start in ((to_a, (1 - odd) * (lats - STEPS)), (to_b, odd * (lats - STEPS))):
        for lev in range(levs):
            for row in range(STEPS):
                out[lev, row] = own[lev, start + row].astype(jnp.bfloat16)
            out[lev, STEPS] = own[lev, lats].astype(jnp.bfloat16)


def obs_kernel(lats, owner, block_row, count, innov, oper, *refs):
    outs, acc = refs[:-1], refs[-1]
    step = pl.program_id(0)
    blocks = oper.shape[0]
    rows = innov.shape[0] // blocks
    fields = 8
    levs = rows // fields

    @pl.when(step == 0)
    def _():
        acc[...] = jnp.zeros_like(acc)

    lane = lax.broadcasted_iota(jnp.int32, (1, innov.shape[1]), 1)
    for i in range(blocks):
        block = step * blocks + i
        seen = (lane < count[block]).astype(jnp.float32).astype(jnp.bfloat16)
        masked = innov[i * rows : (i + 1) * rows, :] * seen
        product = jnp.dot(masked, oper[i], preferred_element_type=jnp.float32)
        spot = owner[block] * lats + block_row[block]
        product = product.astype(jnp.bfloat16).astype(jnp.float32)
        for half in range(acc.shape[1]):
            part = product[:, half * LANES : (half + 1) * LANES]
            acc[spot, half] = acc[spot, half] + part

    def by_field(spot, lev):
        halves = [
            acc[spot, half, pl.ds(lev, fields, stride=levs), :] for half in range(acc.shape[1])
        ]
        return jnp.concatenate(halves, axis=1)

    @pl.when(step == pl.num_programs(0) - 1)
    def _():
        if len(outs) == 2:
            mine = lax.axis_index("lon")
            for out, tile in zip(outs, (mine, 1 - mine)):
                for row in range(lats):
                    for lev in range(levs):
                        value = by_field(tile * lats + row, lev)
                        out[lev, row] = value.astype(out.dtype)
        else:
            (out,) = outs
            for tile in range(out.shape[0]):
                for row in range(lats):
                    for lev in range(levs):
                        out[tile, lev, row] = by_field(tile * lats + row, lev)


def lat_kernel(own, from_a, from_b, _, ext, to_a, to_b):
    levs, lats = own.shape[0], own.shape[1] - 1
    place = lax.axis_index("lat")
    even = lax.rem(place, 2) == 0
    south_in = (place > 0).astype(jnp.float32)
    north_in = (place < lax.axis_size("lat") - 1).astype(jnp.float32)
    south_wind, own_wind, north_wind = lats + 2 * STEPS, lats + 2 * STEPS + 1, lats + 2 * STEPS + 2

    def fill(south, north):
        for lev in range(levs):
            for row in range(STEPS):
                ext[lev, row] = south[lev, row].astype(jnp.float32) * south_in
                ext[lev, STEPS + lats + row] = north[lev, row].astype(jnp.float32) * north_in
            ext[lev, south_wind] = south[lev, STEPS].astype(jnp.float32)
            ext[lev, north_wind] = north[lev, STEPS].astype(jnp.float32)

    @pl.when(even)
    def _():
        fill(from_b, from_a)

    @pl.when(jnp.logical_not(even))
    def _():
        fill(from_a, from_b)

    for lev in range(levs):
        for row in range(lats):
            ext[lev, STEPS + row] = own[lev, row]
        ext[lev, own_wind] = own[lev, lats]
    odd = lax.rem(lax.axis_index("lev"), 2)
    sub = lax.broadcasted_iota(jnp.int32, own.shape[2:], 0)
    outer = lax.rem(sub, lats) >= lats // 2
    for out, down in ((to_a, odd), (to_b, 1 - odd)):
        at = 0
        for d, first, rows in lev_rows(lats):
            lev = down * (d - 1) + (1 - down) * (levs - d)
            for row in range(rows):
                out[at + row] = ext[lev, STEPS + first + row].astype(jnp.bfloat16)
            at += rows
        for d in range(1, STEPS):
            lev = down * (d - 1) + (1 - down) * (levs - d)
            out[at] = ext[lev, own_wind].astype(jnp.bfloat16)
            both = jnp.where(outer, ext[lev, south_wind], ext[lev, north_wind])
            out[at + 1] = both.astype(jnp.bfloat16)
            at += 2


def pack_order(levs, lats, lev_tiles):
    order = [("ext", lev, tile) for lev in range(levs) for tile in range(lats + 2 * STEPS + 3)]
    return order + [("lev", side, tile) for side in range(2) for tile in range(lev_tiles)]


def lev_kernel(ext, from_a, from_b, lev, edges):
    levs, lats = ext.shape[0], ext.shape[1] - 2 * STEPS - 3
    tiles = lev.shape[1]
    place = lax.axis_index("lev")
    even = lax.rem(place, 2) == 0
    below_in = (place > 0).astype(jnp.float32)
    above_in = (place < lax.axis_size("lev") - 1).astype(jnp.float32)

    def fill(below, above):
        for tile in range(tiles):
            lev[0, tile] = below[tile].astype(jnp.float32) * below_in
            lev[1, tile] = above[tile].astype(jnp.float32) * above_in

    @pl.when(even)
    def _():
        fill(from_b, from_a)

    @pl.when(jnp.logical_not(even))
    def _():
        fill(from_a, from_b)

    lane = lax.broadcasted_iota(jnp.int32, (ext.shape[2], LANES), 1)
    total = None
    order = pack_order(levs, lats, tiles)
    for n, (kind, i, tile) in enumerate(order):
        ref = ext if kind == "ext" else lev
        k = n % PER_TILE
        value = jnp.where(lane < GROUP, ref[i, tile, :, 0:LANES], ref[i, tile, :, -LANES:])
        value = pltpu.roll(value, GROUP * k + STEPS, 1)
        total = value if k == 0 else jnp.where(lane // GROUP == k, value, total)
        if k == PER_TILE - 1 or n == len(order) - 1:
            edges[n // PER_TILE] = total.astype(jnp.bfloat16)


def step_kernel(
    diff, vert, ext, lev, west, east, obs_a, obs_b, out_hbm, rows_a, rows_b, result, sem
):
    levs, lats = ext.shape[0], ext.shape[1] - 2 * STEPS - 3
    fields, lons = ext.shape[2], ext.shape[3]
    width = lons + LANES
    tiles = lev.shape[1]
    level_total = vert.shape[0]
    lat_place, lev_place = lax.axis_index("lat"), lax.axis_index("lev")
    south_in = (lat_place > 0).astype(jnp.float32)
    north_in = (lat_place < lax.axis_size("lat") - 1).astype(jnp.float32)
    below_in = (lev_place > 0).astype(jnp.float32)
    above_in = (lev_place < lax.axis_size("lev") - 1).astype(jnp.float32)
    where = {key: n for n, key in enumerate(pack_order(levs, lats, tiles))}
    lane = lax.broadcasted_iota(jnp.int32, (fields, LANES), 1)
    sub = lax.broadcasted_iota(jnp.int32, (fields, width), 0)
    hd = jnp.zeros((fields, width), jnp.float32)
    for f in range(fields):
        hd = jnp.where(sub == f, diff[f], hd)

    starts, at = {}, 0
    for d, first, rows in lev_rows(lats):
        starts[d] = (at, first)
        at += rows
    winds_at = at

    def source(k, j):
        if 0 <= k < levs:
            return ("ext", k, STEPS + j)
        side, d = (0, -k) if k < 0 else (1, k - levs + 1)
        begin, first = starts[d]
        return ("lev", side, begin + j - first)

    def wind_source(k, j, which):
        tile = 0 if j < 0 else (1 if j < lats else 2)
        row = which * lats + j % lats
        if 0 <= k < levs:
            return ("ext", k, lats + 2 * STEPS + tile), row
        side, d = (0, -k) if k < 0 else (1, k - levs + 1)
        return ("lev", side, winds_at + 2 * (d - 1) + (0 if tile == 1 else 1)), row

    opened = {}

    def edge(key):
        n = where[key]
        if n // PER_TILE not in opened:
            value_w = west[n // PER_TILE].astype(jnp.float32)
            opened[n // PER_TILE] = (
                (value_w, value_w)
                if west is east
                else (value_w, east[n // PER_TILE].astype(jnp.float32))
            )
        value_w, value_e = opened[n // PER_TILE]
        shift = (LANES - GROUP * (n % PER_TILE) - STEPS) % LANES
        if value_w is value_e:
            return pltpu.roll(value_w, shift, 1)
        return jnp.where(
            lane < LANES // 2, pltpu.roll(value_e, shift, 1), pltpu.roll(value_w, shift, 1)
        )

    def main(key):
        kind, i, tile = key
        return (ext if kind == "ext" else lev)[i, tile]

    def distance(k, j):
        dk = -k if k < 0 else max(0, k - levs + 1)
        dj = -j if j < 0 else max(0, j - lats + 1)
        return dk + dj

    def spot(k, j):
        return (k + STEPS) * (lats + 2 * STEPS) + j + STEPS

    cells = [(k, j) for k in range(-STEPS, levs + STEPS) for j in range(-STEPS, lats + STEPS)]
    for k, j in cells:
        if distance(k, j) <= STEPS:
            key = source(k, j)
            rows_a[spot(k, j), :, 0:lons] = main(key)
            rows_a[spot(k, j), :, lons:width] = edge(key)

    wind_edges = {}

    def wind(k, j, which):
        key, row = wind_source(k, j, which)
        if key not in wind_edges:
            wind_edges[key] = jnp.concatenate([main(key), edge(key)], axis=1)
        return wind_edges[key][row : row + 1, :]

    up, down = {}, {}
    for k in range(1 - STEPS, levs + STEPS - 1):
        level = lev_place * levs + k
        last = jnp.minimum(jnp.maximum(level, 0), level_total - 1)
        before = jnp.minimum(jnp.maximum(level - 1, 0), level_total - 1)
        up[k] = jnp.where(level < level_total - 1, vert[last], 0.0)
        down[k] = jnp.where(level >= 1, vert[before], 0.0)

    source_rows, target_rows = rows_a, rows_b
    copies = []
    for n in range(1, STEPS + 1):
        for k, j in cells:
            if distance(k, j) > STEPS - n:
                continue
            a = source_rows[spot(k, j)]
            u, w = wind(k, j, 0), wind(k, j, 1)
            north = source_rows[spot(k, j + 1)]
            east_part = (u + hd) * a
            new = a * (1.0 - up[k] - down[k] - u - w - 4.0 * hd)
            new = new + pltpu.roll(east_part, width - 1, 1) + hd * pltpu.roll(a, 1, 1)
            new = new + (wind(k, j + 1, 1) + hd) * north + hd * source_rows[spot(k, j - 1)]
            new = new + up[k] * source_rows[spot(k + 1, j)]
            new = new + down[k] * source_rows[spot(k - 1, j)]
            if k < 0:
                new = new * below_in
            elif k >= levs:
                new = new * above_in
            if j < 0:
                new = new * south_in
            elif j >= lats:
                new = new * north_in
            if n < STEPS:
                target_rows[spot(k, j)] = new
            else:
                obs = obs_a[k, j]
                if obs_b is not None:
                    obs = obs + obs_b[k, j].astype(jnp.float32)
                result[k, j] = new[:, 0:lons] + obs
        source_rows, target_rows = target_rows, source_rows
    for f in range(fields):
        copies.append(pltpu.make_async_copy(result.at[:, :, f, :], out_hbm.at[f], sem.at[f]))
        copies[-1].start()
    for copy in copies:
        copy.wait()


def on_device(
    adjoint_in,
    courant_lon,
    courant_lat,
    horiz_diff,
    vert_diff,
    innovations,
    obs_operator,
    owner_tile,
    block_row,
    obs_count,
):
    fields, levs, lats, lons = adjoint_in.shape
    blocks, _, _, obs_rows = innovations.shape
    n_lon, n_lat, n_lev = (lax.axis_size(axis) for axis in ("lon", "lat", "lev"))
    f32, bf16 = jnp.float32, jnp.bfloat16
    assert lats >= STEPS and levs >= STEPS and lons % LANES == 0 and fields == 2 * lats

    tile = (fields, lons)
    smalls = (owner_tile[:, 0], block_row, obs_count)
    inputs = (adjoint_in, courant_lon, courant_lat) + smalls
    own, to_lat_a, to_lat_b, *smalls = pl.pallas_call(
        load_kernel,
        out_shape=(
            jax.ShapeDtypeStruct((levs, lats + 1) + tile, f32),
            jax.ShapeDtypeStruct((levs, STEPS + 1) + tile, bf16),
            jax.ShapeDtypeStruct((levs, STEPS + 1) + tile, bf16),
        )
        + tuple(jax.ShapeDtypeStruct(x.shape, x.dtype) for x in smalls),
        in_specs=[HBM] * 6,
        out_specs=(VMEM,) * 6,
        scratch_shapes=[pltpu.SemaphoreType.DMA((fields + 5,))],
        cost_estimate=cost(1, 64 << 20),
        compiler_params=PARAMS,
        name="load",
    )(*(pltpu.with_memory_space_constraint(x, pltpu.HBM) for x in inputs))
    from_lat_a = lax.ppermute(to_lat_a, ("lat", "lev"), pair_up(n_lat, 0, n_lev, True))
    from_lat_b = lax.ppermute(to_lat_b, ("lat", "lev"), pair_up(n_lat, 1, n_lev, True))

    group = 8
    while blocks % group:
        group //= 2
    rows = fields * levs
    targets = n_lon * lats
    if n_lon == 2:
        obs_out = (
            jax.ShapeDtypeStruct((levs, lats) + tile, f32),
            jax.ShapeDtypeStruct((levs, lats) + tile, bf16),
        )
    else:
        obs_out = (jax.ShapeDtypeStruct((n_lon, levs, lats) + tile, f32),)
    obs = pl.pallas_call(
        functools.partial(obs_kernel, lats),
        out_shape=obs_out,
        grid_spec=pltpu.PrefetchScalarGridSpec(
            num_scalar_prefetch=3,
            grid=(blocks // group,),
            in_specs=[
                pl.BlockSpec((group * rows, obs_rows), lambda i, *_: (i, 0)),
                pl.BlockSpec((group, obs_rows, lons), lambda i, *_: (i, 0, 0)),
            ],
            out_specs=(VMEM,) * len(obs_out),
            scratch_shapes=[pltpu.VMEM((targets, lons // LANES, rows, LANES), f32)],
        ),
        cost_estimate=cost(2 * blocks * rows * obs_rows * lons, 12 << 20),
        compiler_params=PARAMS,
        name="obs",
    )(
        *smalls,
        innovations.reshape(blocks * rows, obs_rows),
        obs_operator,
    )

    lev_tiles = sum(rows for _, _, rows in lev_rows(lats)) + 2 * (STEPS - 1)
    ext_tiles = lats + 2 * STEPS + 3
    ext, to_lev_a, to_lev_b = pl.pallas_call(
        lat_kernel,
        out_shape=(
            jax.ShapeDtypeStruct((levs, ext_tiles) + tile, f32),
            jax.ShapeDtypeStruct((lev_tiles,) + tile, bf16),
            jax.ShapeDtypeStruct((lev_tiles,) + tile, bf16),
        ),
        in_specs=[VMEM] * 3 + [ANY],
        out_specs=(VMEM,) * 3,
        cost_estimate=cost(1, 1 << 20),
        compiler_params=PARAMS,
        name="extend_lat",
    )(own, from_lat_a, from_lat_b, obs[0])
    from_lev_b = lax.ppermute(to_lev_b, ("lat", "lev"), pair_up(n_lev, 1, n_lat, False))
    from_lev_a = lax.ppermute(to_lev_a, ("lat", "lev"), pair_up(n_lev, 0, n_lat, False))

    if n_lon == 2:
        obs_own = obs[0]
        obs_from = lax.ppermute(obs[1], "lon", [(0, 1), (1, 0)])
    else:
        flat = obs[0].reshape(-1, lons)
        obs_own = lax.psum_scatter(flat, "lon", scatter_dimension=0, tiled=True)
        obs_own = obs_own.reshape((levs, lats) + tile)
        obs_from = None

    packed = -(-(levs * ext_tiles + 2 * lev_tiles) // PER_TILE)
    lev, edges = pl.pallas_call(
        lev_kernel,
        out_shape=(
            jax.ShapeDtypeStruct((2, lev_tiles) + tile, f32),
            jax.ShapeDtypeStruct((packed, fields, LANES), bf16),
        ),
        in_specs=[VMEM] * 3,
        out_specs=(VMEM,) * 2,
        cost_estimate=cost(1, 1 << 20),
        compiler_params=PARAMS,
        name="extend_lev",
    )(ext, from_lev_a, from_lev_b)
    east_ring = [(i, (i + 1) % n_lon) for i in range(n_lon)]
    west = lax.ppermute(edges, "lon", east_ring)
    halos = [west]
    if n_lon > 2:
        halos.append(lax.ppermute(edges, "lon", [(b, a) for a, b in east_ring]))
    sums = [obs_own] if obs_from is None else [obs_own, obs_from]

    def run(diff, vert, ext_ref, lev_ref, *refs):
        halo_refs, rest = refs[: len(halos)], refs[len(halos) :]
        obs_refs, rest = rest[: len(sums)], rest[len(sums) :]
        step_kernel(
            diff,
            vert,
            ext_ref,
            lev_ref,
            halo_refs[0],
            halo_refs[-1],
            obs_refs[0],
            obs_refs[1] if len(sums) == 2 else None,
            *rest,
        )

    grid_rows = (levs + 2 * STEPS) * (lats + 2 * STEPS)
    return pl.pallas_call(
        run,
        out_shape=jax.ShapeDtypeStruct(adjoint_in.shape, f32),
        in_specs=[SMEM, SMEM] + [VMEM] * (2 + len(halos) + len(sums)),
        out_specs=ANY,
        scratch_shapes=[
            pltpu.VMEM((grid_rows, fields, lons + LANES), f32),
            pltpu.VMEM((grid_rows, fields, lons + LANES), f32),
            pltpu.VMEM((levs, lats) + tile, f32),
            pltpu.SemaphoreType.DMA((fields,)),
        ],
        cost_estimate=cost(1, 4 << 20),
        compiler_params=PARAMS,
        name="sub_steps",
    )(horiz_diff, vert_diff, ext, lev, *halos, *sums)


def solution(mesh):
    in_specs = (
        P(None, "lev", "lat", "lon"),
        P("lev", "lat", "lon"),
        P("lev", "lat", "lon"),
        P(),
        P(),
        P(("lon", "lat"), None, "lev", None),
        P(("lon", "lat"), None, None),
        P(("lon", "lat"), None),
        P(("lon", "lat")),
        P(("lon", "lat")),
    )
    out_specs = P(None, "lev", "lat", "lon")
    return jax.shard_map(
        on_device, mesh=mesh, in_specs=in_specs, out_specs=out_specs, check_vma=False
    )
```

```python
import functools

import jax
import jax.numpy as jnp
from jax import lax
from jax.experimental import pallas as pl
from jax.experimental.pallas import tpu as pltpu
from jax.sharding import PartitionSpec as P

STEPS = 3
LANES = 128
GROUP = 16
PER_TILE = LANES // GROUP
VMEM = pl.BlockSpec(memory_space=pltpu.VMEM)
SMEM = pl.BlockSpec(memory_space=pltpu.SMEM)
ANY = pl.BlockSpec(memory_space=pl.ANY)
HBM = pl.BlockSpec(memory_space=pltpu.HBM)


PARAMS = pltpu.CompilerParams(vmem_limit_bytes=12 << 20)


def cost(flops, nbytes):
    return pl.CostEstimate(flops=flops, bytes_accessed=nbytes, transcendentals=0)


def pair_up(sizes, axis, phase, shift=0):
    n_lon, n_lat, n_lev = sizes
    pairs = []
    for lon in range(n_lon):
        for lat in range(n_lat):
            for lev in range(n_lev):
                to = [(lon + shift) % n_lon, lat, lev]
                if axis:
                    mate = to[axis] + (1 if to[axis] % 2 == phase else -1)
                    if 0 <= mate < sizes[axis]:
                        to[axis] = mate
                    elif shift % n_lon == 0:
                        to[3 - axis] ^= 1
                        if to[3 - axis] >= sizes[3 - axis]:
                            continue
                ends = [(p * n_lat + q) * n_lev + r for p, q, r in ((lon, lat, lev), to)]
                pairs.append(tuple(ends))
    return pairs


def send(x, pairs):
    return lax.ppermute(x, ("lon", "lat", "lev"), pairs)


def pack(tiles, out, at):
    total = None
    for n, value in enumerate(tiles):
        k = n % PER_TILE
        lane = lax.broadcasted_iota(jnp.int32, (value.shape[0], LANES), 1)
        value = jnp.where(lane < LANES // 2, value[:, 0:LANES], value[:, -LANES:])
        if k:
            value = pltpu.roll(value, GROUP * k, 1)
            value = jnp.where((lane + STEPS) % LANES // GROUP == k, value, total)
        total = value
        if k == PER_TILE - 1 or n == len(tiles) - 1:
            total = jnp.where(lane % GROUP < GROUP // 2, total, pltpu.roll(total, GROUP, 1))
            out[at + n // PER_TILE] = total.astype(out.dtype)


def lev_rows(lat_cells):
    return [(d, -(STEPS - d), lat_cells + 2 * (STEPS - d)) for d in range(1, STEPS + 1)]


def load_kernel(adj, wind_u, wind_w, *refs):
    small, (own, to_a, to_b), small_out, sem = refs[:3], refs[3:6], refs[6:9], refs[9]
    fields, levs, lats = adj.shape[:3]
    copies = [
        pltpu.make_async_copy(adj.at[f], own.at[:, 0:lats, f, :], sem.at[f]) for f in range(fields)
    ]
    copies.append(pltpu.make_async_copy(wind_u, own.at[:, lats, 0:lats, :], sem.at[fields]))
    copies.append(
        pltpu.make_async_copy(wind_w, own.at[:, lats, lats : 2 * lats, :], sem.at[fields + 1])
    )
    for n, (source, target) in enumerate(zip(small, small_out)):
        copies.append(pltpu.make_async_copy(source, target, sem.at[fields + 2 + n]))
    for copy in copies:
        copy.start()
    for copy in copies:
        copy.wait()
    odd = lax.rem(lax.axis_index("lat"), 2)
    for out, start in ((to_a, (1 - odd) * (lats - STEPS)), (to_b, odd * (lats - STEPS))):
        for lev in range(levs):
            for row in range(STEPS):
                out[lev, row] = own[lev, start + row].astype(jnp.bfloat16)
            out[lev, STEPS] = own[lev, lats].astype(jnp.bfloat16)


def obs_kernel(lats, owner, block_row, count, innov, oper, *refs):
    outs, (lhs, rhs, acc, sem) = refs[:-4], refs[-4:]
    blocks = oper.shape[0]
    rows = innov.shape[0] // blocks
    fields = 2 * lats
    levs = rows // fields
    chunks = sem.shape[1]
    per = blocks // chunks
    copies = []
    for n in range(chunks):
        some, some_rows = pl.ds(n * per, per), pl.ds(n * per * rows, per * rows)
        copies.append(
            (
                pltpu.make_async_copy(innov.at[some_rows], lhs.at[some_rows], sem.at[0, n]),
                pltpu.make_async_copy(oper.at[some], rhs.at[some], sem.at[1, n]),
            )
        )
        for copy in copies[-1]:
            copy.start()
    acc[...] = jnp.zeros_like(acc)
    lane = lax.broadcasted_iota(jnp.int32, (1, innov.shape[1]), 1)
    for block in range(blocks):
        if block % per == 0:
            for copy in copies[block // per]:
                copy.wait()
        seen = (lane < count[block]).astype(jnp.float32).astype(jnp.bfloat16)
        masked = lhs[block * rows : (block + 1) * rows, :] * seen
        product = jnp.dot(masked, rhs[block], preferred_element_type=jnp.float32)
        spot = owner[block] * lats + block_row[block]
        product = product.astype(jnp.bfloat16).astype(jnp.float32)
        for half in range(acc.shape[1]):
            part = product[:, half * LANES : (half + 1) * LANES]
            acc[spot, half] = acc[spot, half] + part

    def by_field(spot, lev):
        halves = [
            acc[spot, half, pl.ds(lev, fields, stride=levs), :] for half in range(acc.shape[1])
        ]
        return jnp.concatenate(halves, axis=1)

    if len(outs) == 2:
        mine = lax.axis_index("lon")
        for out, tile in zip(outs, (mine, 1 - mine)):
            for row in range(lats):
                for lev in range(levs):
                    out[lev, row] = by_field(tile * lats + row, lev).astype(out.dtype)
    else:
        (out,) = outs
        for tile in range(out.shape[0]):
            for row in range(lats):
                for lev in range(levs):
                    out[tile, lev, row] = by_field(tile * lats + row, lev)


def lat_kernel(own, from_a, from_b, obs, ext, to_a, to_b, edges, edges_a, edges_b):
    levs, lats = own.shape[0], own.shape[1] - 1
    place = lax.axis_index("lat")
    even = lax.rem(place, 2) == 0
    south_in = (place > 0).astype(jnp.float32)
    north_in = (place < lax.axis_size("lat") - 1).astype(jnp.float32)
    south_wind, own_wind, north_wind = lats + 2 * STEPS, lats + 2 * STEPS + 1, lats + 2 * STEPS + 2

    def fill(south, north):
        for lev in range(levs):
            for row in range(STEPS):
                ext[lev, row] = south[lev, row].astype(jnp.float32) * south_in
                ext[lev, STEPS + lats + row] = north[lev, row].astype(jnp.float32) * north_in
            ext[lev, south_wind] = south[lev, STEPS].astype(jnp.float32)
            ext[lev, north_wind] = north[lev, STEPS].astype(jnp.float32)

    @pl.when(even)
    def _():
        fill(from_b, from_a)

    @pl.when(jnp.logical_not(even))
    def _():
        fill(from_a, from_b)

    for lev in range(levs):
        for row in range(lats):
            ext[lev, STEPS + row] = own[lev, row]
        ext[lev, own_wind] = own[lev, lats]
    odd = lax.rem(lax.axis_index("lev"), 2)
    sub = lax.broadcasted_iota(jnp.int32, own.shape[2:], 0)
    outer = lax.rem(sub, lats) >= lats // 2
    for out, packed, down in ((to_a, edges_a, odd), (to_b, edges_b, 1 - odd)):
        tiles = []
        for d, first, rows in lev_rows(lats):
            lev = down * (d - 1) + (1 - down) * (levs - d)
            tiles += [ext[lev, STEPS + first + row] for row in range(rows)]
        for d in range(1, STEPS):
            lev = down * (d - 1) + (1 - down) * (levs - d)
            tiles.append(ext[lev, own_wind])
            tiles.append(jnp.where(outer, ext[lev, south_wind], ext[lev, north_wind]))
        for n, value in enumerate(tiles):
            out[n] = value.astype(jnp.bfloat16)
        pack(tiles, packed, 0)
    at = 0
    if edges.shape[0] > -(-levs * ext.shape[1] // PER_TILE):
        for lev in range(levs):
            for row in range(lats):
                for half in range(ext.shape[3] // LANES):
                    edges[at] = obs[lev, row, :, half * LANES : (half + 1) * LANES]
                    at += 1
    pack([ext[lev, n] for lev in range(levs) for n in range(ext.shape[1])], edges, at)


class Steps:
    def __init__(self, levs, lats, lev_tiles, level_total):
        self.levs, self.lats, self.level_total = levs, lats, level_total
        keys = [("ext", k, tile) for k in range(levs) for tile in range(lats + 2 * STEPS + 3)]
        keys += [("lev", side, tile) for side in range(2) for tile in range(lev_tiles)]
        self.order = {key: n for n, key in enumerate(keys)}
        self.starts, at = {}, 0
        for d, first, rows in lev_rows(lats):
            self.starts[d] = at - first
            at += rows
        self.winds_at = at
        self.cells = [
            (k, j) for k in range(-STEPS, levs + STEPS) for j in range(-STEPS, lats + STEPS)
        ]

    def distance(self, k, j):
        return max(-k, 0, k - self.levs + 1) + max(-j, 0, j - self.lats + 1)

    def spot(self, k, j):
        return (k + STEPS) * (self.lats + 2 * STEPS) + j + STEPS

    def side(self, k):
        return (0, -k) if k < 0 else (1, k - self.levs + 1)

    def source(self, k, j):
        if 0 <= k < self.levs:
            return ("ext", k, STEPS + j)
        side, d = self.side(k)
        return ("lev", side, self.starts[d] + j)

    def wind_source(self, k, j, which):
        tile = 0 if j < 0 else (1 if j < self.lats else 2)
        row = which * self.lats + j % self.lats
        if 0 <= k < self.levs:
            return ("ext", k, self.lats + 2 * STEPS + tile), row
        side, d = self.side(k)
        return ("lev", side, self.winds_at + 2 * (d - 1) + (0 if tile == 1 else 1)), row

    def run(self, diff, vert, shape, first_rows, wind, buffers, emit):
        levs, lats = self.levs, self.lats
        width = shape[1]
        lat_place, lev_place = lax.axis_index("lat"), lax.axis_index("lev")
        south_in = (lat_place > 0).astype(jnp.float32)
        north_in = (lat_place < lax.axis_size("lat") - 1).astype(jnp.float32)
        below_in = (lev_place > 0).astype(jnp.float32)
        above_in = (lev_place < lax.axis_size("lev") - 1).astype(jnp.float32)
        sub = lax.broadcasted_iota(jnp.int32, shape, 0)
        hd = jnp.zeros(shape, jnp.float32)
        for f in range(shape[0]):
            hd = jnp.where(sub == f, diff[f], hd)
        up, down = {}, {}
        for k in range(1 - STEPS, levs + STEPS - 1):
            level = lev_place * levs + k
            last = jnp.minimum(jnp.maximum(level, 0), self.level_total - 1)
            before = jnp.minimum(jnp.maximum(level - 1, 0), self.level_total - 1)
            up[k] = jnp.where(level < self.level_total - 1, vert[last], 0.0)
            down[k] = jnp.where(level >= 1, vert[before], 0.0)
        rows = first_rows
        for n in range(1, STEPS + 1):
            target = None if n == STEPS else buffers[(n - 1) % 2]
            for k, j in self.cells:
                if self.distance(k, j) > STEPS - n:
                    continue
                a = rows(k, j)
                u, w = wind(k, j, 0), wind(k, j, 1)
                new = a * (1.0 - up[k] - down[k] - u - w - 4.0 * hd)
                new = new + pltpu.roll((u + hd) * a, width - 1, 1) + hd * pltpu.roll(a, 1, 1)
                new = new + (wind(k, j + 1, 1) + hd) * rows(k, j + 1) + hd * rows(k, j - 1)
                new = new + up[k] * rows(k + 1, j) + down[k] * rows(k - 1, j)
                if k < 0:
                    new = new * below_in
                elif k >= levs:
                    new = new * above_in
                if j < 0:
                    new = new * south_in
                elif j >= lats:
                    new = new * north_in
                if target is None:
                    emit(k, j, new)
                else:
                    target[self.spot(k, j)] = new
            if target is not None:
                rows = functools.partial(lambda ref, k, j: ref[self.spot(k, j)], target)


EAST_END = LANES // 2
FIRST_AT = EAST_END + GROUP


def sides(low, high):
    place = lax.axis_index("lev")
    even = lax.rem(place, 2) == 0
    below_in = (place > 0).astype(jnp.float32)
    above_in = (place < lax.axis_size("lev") - 1).astype(jnp.float32)
    below, above = jnp.where(even, high, low), jnp.where(even, low, high)
    return below * below_in, above * above_in


def main_kernel(diff, vert, ext, from_a, from_b, result, edge_rows, lev, rows_a, rows_b):
    levs, lats = ext.shape[0], ext.shape[1] - 2 * STEPS - 3
    for tile in range(lev.shape[1]):
        low, high = from_a[tile].astype(jnp.float32), from_b[tile].astype(jnp.float32)
        lev[0, tile], lev[1, tile] = sides(low, high)
    steps = Steps(levs, lats, lev.shape[1], vert.shape[0])
    refs = {"ext": ext, "lev": lev}

    def first_rows(k, j):
        kind, i, tile = steps.source(k, j)
        return refs[kind][i, tile]

    def wind(k, j, which):
        (kind, i, tile), row = steps.wind_source(k, j, which)
        return refs[kind][i, tile, row : row + 1, :]

    def emit(k, j, new):
        result[k, j] = new

    steps.run(diff, vert, ext.shape[2:], first_rows, wind, (rows_a, rows_b), emit)
    lane = lax.broadcasted_iota(jnp.int32, edge_rows.shape[1:], 1)
    for n, (kind, i, tile) in enumerate(steps.order):
        first = pltpu.roll(refs[kind][i, tile, :, 0:LANES], FIRST_AT, 1)
        last = pltpu.roll(refs[kind][i, tile, :, -LANES:], EAST_END, 1)
        edge_rows[n] = jnp.where(lane < EAST_END, last, first)


def edge_kernel(levs, lats, lev_tiles, n_ways, diff, vert, main, own_rows, obs, *refs):
    halos, (out, edge_rows, rows_a, rows_b, result, sem) = refs[: 3 * n_ways], refs[3 * n_ways :]
    fields, lons = main.shape[2:]
    parts = lons // LANES
    steps = Steps(levs, lats, lev_tiles, vert.shape[0])
    lane = lax.broadcasted_iota(jnp.int32, (fields, LANES), 1)
    in_halo = (lane >= EAST_END) & (lane < FIRST_AT)
    ext_rows = len(steps.order) - 2 * lev_tiles
    obs_at = levs * lats * parts if n_ways == 1 else 0

    def packed(which, n):
        tiles = [halos[3 * way + which][n].astype(jnp.float32) for way in range(n_ways)]
        return jnp.where(lane % GROUP < GROUP // 2, tiles[-1], tiles[0])

    def unpack(tile, at, count):
        for k in range(count):
            halo = pltpu.roll(tile, (EAST_END - GROUP * k) % LANES, 1)
            edge_rows[at + k] = jnp.where(in_halo, halo, own_rows[at + k])

    for at in range(0, ext_rows, PER_TILE):
        unpack(packed(0, obs_at + at // PER_TILE), at, min(PER_TILE, ext_rows - at))
    for at in range(0, lev_tiles, PER_TILE):
        both = sides(packed(1, at // PER_TILE), packed(2, at // PER_TILE))
        for side, tile in enumerate(both):
            start = ext_rows + side * lev_tiles + at
            unpack(tile, start, min(PER_TILE, lev_tiles - at))

    def first_rows(k, j):
        return edge_rows[steps.order[steps.source(k, j)]]

    def wind(k, j, which):
        key, row = steps.wind_source(k, j, which)
        return edge_rows[steps.order[key], row : row + 1, :]

    def total(k, j, part):
        value = obs[k, j, :, part * LANES : (part + 1) * LANES]
        if n_ways == 1:
            value = value + halos[0][(k * lats + j) * parts + part].astype(jnp.float32)
        return value

    def emit(k, j, new):
        first = pltpu.roll(new, LANES - FIRST_AT, 1)
        last = pltpu.roll(new, LANES - EAST_END, 1)
        for part in range(parts):
            value = main[k, j, :, part * LANES : (part + 1) * LANES]
            if part == 0:
                value = jnp.where(lane < STEPS, first, value)
            if part == parts - 1:
                value = jnp.where(lane >= LANES - STEPS, last, value)
            result[k, j, :, part * LANES : (part + 1) * LANES] = value + total(k, j, part)

    steps.run(diff, vert, (fields, LANES), first_rows, wind, (rows_a, rows_b), emit)
    copies = [
        pltpu.make_async_copy(result.at[:, :, f, :], out.at[f], sem.at[f]) for f in range(fields)
    ]
    for copy in copies:
        copy.start()
    for copy in copies:
        copy.wait()


def on_device(
    adjoint_in,
    courant_lon,
    courant_lat,
    horiz_diff,
    vert_diff,
    innovations,
    obs_operator,
    owner_tile,
    block_row,
    obs_count,
):
    fields, levs, lats, lons = adjoint_in.shape
    blocks, _, _, obs_rows = innovations.shape
    n_lon, n_lat, n_lev = (lax.axis_size(axis) for axis in ("lon", "lat", "lev"))
    f32, bf16 = jnp.float32, jnp.bfloat16
    assert lats >= STEPS and levs >= STEPS and lons % LANES == 0 and fields == 2 * lats

    tile = (fields, lons)
    smalls = (owner_tile[:, 0], block_row, obs_count)
    inputs = (adjoint_in, courant_lon, courant_lat) + smalls
    own, to_lat_a, to_lat_b, *smalls = pl.pallas_call(
        load_kernel,
        out_shape=(
            jax.ShapeDtypeStruct((levs, lats + 1) + tile, f32),
            jax.ShapeDtypeStruct((levs, STEPS + 1) + tile, bf16),
            jax.ShapeDtypeStruct((levs, STEPS + 1) + tile, bf16),
        )
        + tuple(jax.ShapeDtypeStruct(x.shape, x.dtype) for x in smalls),
        in_specs=[HBM] * 6,
        out_specs=(VMEM,) * 6,
        scratch_shapes=[pltpu.SemaphoreType.DMA((fields + 5,))],
        cost_estimate=cost(1, 64 << 20),
        compiler_params=PARAMS,
        name="load",
    )(*(pltpu.with_memory_space_constraint(x, pltpu.HBM) for x in inputs))
    sizes = (n_lon, n_lat, n_lev)
    from_lat_a = send(to_lat_a, pair_up(sizes, 1, 0))
    from_lat_b = send(to_lat_b, pair_up(sizes, 1, 1))

    chunks = 8
    while blocks % chunks:
        chunks //= 2
    rows = fields * levs
    targets = n_lon * lats
    if n_lon == 2:
        obs_out = (
            jax.ShapeDtypeStruct((levs, lats) + tile, f32),
            jax.ShapeDtypeStruct((levs, lats) + tile, bf16),
        )
    else:
        obs_out = (jax.ShapeDtypeStruct((n_lon, levs, lats) + tile, f32),)
    obs = pl.pallas_call(
        functools.partial(obs_kernel, lats),
        out_shape=obs_out,
        in_specs=[SMEM] * 3 + [HBM] * 2,
        out_specs=(VMEM,) * len(obs_out),
        scratch_shapes=[
            pltpu.VMEM((blocks * rows, obs_rows), bf16),
            pltpu.VMEM(obs_operator.shape, bf16),
            pltpu.VMEM((targets, lons // LANES, rows, LANES), f32),
            pltpu.SemaphoreType.DMA((2, chunks)),
        ],
        cost_estimate=cost(2 * blocks * rows * obs_rows * lons, 12 << 20),
        compiler_params=PARAMS,
        name="obs",
    )(
        *smalls,
        pltpu.with_memory_space_constraint(
            innovations.reshape(blocks * rows, obs_rows), pltpu.HBM
        ),
        pltpu.with_memory_space_constraint(obs_operator, pltpu.HBM),
    )

    lev_tiles = sum(rows for _, _, rows in lev_rows(lats)) + 2 * (STEPS - 1)
    ext_tiles = lats + 2 * STEPS + 3
    ext_packed, lev_packed = -(-levs * ext_tiles // PER_TILE), -(-lev_tiles // PER_TILE)
    obs_tiles = levs * lats * (lons // LANES) if n_lon == 2 else 0
    lane_tile = (fields, LANES)
    ext, to_lev_a, to_lev_b, edges, edges_a, edges_b = pl.pallas_call(
        lat_kernel,
        out_shape=(
            jax.ShapeDtypeStruct((levs, ext_tiles) + tile, f32),
            jax.ShapeDtypeStruct((lev_tiles,) + tile, bf16),
            jax.ShapeDtypeStruct((lev_tiles,) + tile, bf16),
            jax.ShapeDtypeStruct((obs_tiles + ext_packed,) + lane_tile, bf16),
            jax.ShapeDtypeStruct((lev_packed,) + lane_tile, bf16),
            jax.ShapeDtypeStruct((lev_packed,) + lane_tile, bf16),
        ),
        in_specs=[VMEM] * 4,
        out_specs=(VMEM,) * 6,
        cost_estimate=cost(1, 1 << 20),
        compiler_params=PARAMS,
        name="extend_lat",
    )(own, from_lat_a, from_lat_b, obs[-1])
    from_lev_b = send(to_lev_b, pair_up(sizes, 2, 1))
    from_lev_a = send(to_lev_a, pair_up(sizes, 2, 0))
    ways = (1,) if n_lon == 2 else (1, -1)
    halos = []
    for way in ways:
        halos.append(send(edges, pair_up(sizes, 0, 0, way)))
        halos.append(send(edges_a, pair_up(sizes, 2, 0, way)))
        halos.append(send(edges_b, pair_up(sizes, 2, 1, way)))
    if n_lon == 2:
        obs_own = obs[0]
    else:
        flat = obs[0].reshape(-1, lons)
        obs_own = lax.psum_scatter(flat, "lon", scatter_dimension=0, tiled=True)
        obs_own = obs_own.reshape((levs, lats) + tile)

    grid_rows = (levs + 2 * STEPS) * (lats + 2 * STEPS)
    edge_shape = (levs * ext_tiles + 2 * lev_tiles,) + lane_tile
    main, edge_rows = pl.pallas_call(
        main_kernel,
        out_shape=(
            jax.ShapeDtypeStruct((levs, lats) + tile, f32),
            jax.ShapeDtypeStruct(edge_shape, f32),
        ),
        in_specs=[SMEM] * 2 + [VMEM] * 3,
        out_specs=(VMEM,) * 2,
        scratch_shapes=[pltpu.VMEM((2, lev_tiles) + tile, f32)]
        + [pltpu.VMEM((grid_rows,) + tile, f32)] * 2,
        cost_estimate=cost(1, 8 << 20),
        compiler_params=PARAMS,
        name="sub_steps",
    )(horiz_diff, vert_diff, ext, from_lev_a, from_lev_b)
    return pl.pallas_call(
        functools.partial(edge_kernel, levs, lats, lev_tiles, len(ways)),
        out_shape=jax.ShapeDtypeStruct(adjoint_in.shape, f32),
        in_specs=[SMEM] * 2 + [VMEM] * (3 + len(halos)),
        out_specs=ANY,
        scratch_shapes=[
            pltpu.VMEM(edge_shape, f32),
            pltpu.VMEM((grid_rows, fields, LANES), f32),
            pltpu.VMEM((grid_rows, fields, LANES), f32),
            pltpu.VMEM((levs, lats) + tile, f32),
            pltpu.SemaphoreType.DMA((fields,)),
        ],
        cost_estimate=cost(1, 1 << 20),
        compiler_params=PARAMS,
        name="edges",
    )(horiz_diff, vert_diff, main, edge_rows, obs_own, *halos)


def solution(mesh):
    in_specs = (
        P(None, "lev", "lat", "lon"),
        P("lev", "lat", "lon"),
        P("lev", "lat", "lon"),
        P(),
        P(),
        P(("lon", "lat"), None, "lev", None),
        P(("lon", "lat"), None, None),
        P(("lon", "lat"), None),
        P(("lon", "lat")),
        P(("lon", "lat")),
    )
    out_specs = P(None, "lev", "lat", "lon")
    return jax.shard_map(
        on_device, mesh=mesh, in_specs=in_specs, out_specs=out_specs, check_vma=False
    )
```

```python
import functools

import jax
import jax.numpy as jnp
from jax import lax
from jax.experimental import pallas as pl
from jax.experimental.pallas import tpu as pltpu
from jax.sharding import PartitionSpec as P

STEPS = 3
LANES = 128
GROUP = 16
PER_TILE = LANES // GROUP
BITS = 4
PIECE = 1 << BITS
SHARES = (1,) * 3
VMEM = pl.BlockSpec(memory_space=pltpu.VMEM)
SMEM = pl.BlockSpec(memory_space=pltpu.SMEM)
ANY = pl.BlockSpec(memory_space=pl.ANY)
HBM = pl.BlockSpec(memory_space=pltpu.HBM)


PARAMS = pltpu.CompilerParams(vmem_limit_bytes=12 << 20)


def cost(flops, nbytes):
    return pl.CostEstimate(flops=flops, bytes_accessed=nbytes, transcendentals=0)


def pair_up(sizes, axis, phase, shift=0):
    n_lon, n_lat, n_lev = sizes
    pairs = []
    for lon in range(n_lon):
        for lat in range(n_lat):
            for lev in range(n_lev):
                to = [(lon + shift) % n_lon, lat, lev]
                if axis:
                    mate = to[axis] + (1 if to[axis] % 2 == phase else -1)
                    if 0 <= mate < sizes[axis]:
                        to[axis] = mate
                    elif shift % n_lon == 0:
                        to[3 - axis] ^= 1
                        if to[3 - axis] >= sizes[3 - axis]:
                            continue
                ends = [(p * n_lat + q) * n_lev + r for p, q, r in ((lon, lat, lev), to)]
                pairs.append(tuple(ends))
    return pairs


def send(x, pairs):
    return lax.ppermute(x, ("lon", "lat", "lev"), pairs)


def pack(tiles, out, at):
    total = None
    for n, value in enumerate(tiles):
        k = n % PER_TILE
        lane = lax.broadcasted_iota(jnp.int32, (value.shape[0], LANES), 1)
        value = jnp.where(lane < LANES // 2, value[:, 0:LANES], value[:, -LANES:])
        if k:
            value = pltpu.roll(value, GROUP * k, 1)
            value = jnp.where((lane + STEPS) % LANES // GROUP == k, value, total)
        total = value
        if k == PER_TILE - 1 or n == len(tiles) - 1:
            total = jnp.where(lane % GROUP < GROUP // 2, total, pltpu.roll(total, GROUP, 1))
            out[at + n // PER_TILE] = total.astype(out.dtype)


def lev_rows(lat_cells):
    return [(d, -(STEPS - d), lat_cells + 2 * (STEPS - d)) for d in range(1, STEPS + 1)]


def load_kernel(adj, wind_u, wind_w, *refs):
    small, (own, to_a, to_b), small_out, sem = refs[:3], refs[3:6], refs[6:9], refs[9]
    fields, levs, lats = adj.shape[:3]
    copies = [
        pltpu.make_async_copy(adj.at[f], own.at[:, 0:lats, f, :], sem.at[f]) for f in range(fields)
    ]
    copies.append(pltpu.make_async_copy(wind_u, own.at[:, lats, 0:lats, :], sem.at[fields]))
    copies.append(
        pltpu.make_async_copy(wind_w, own.at[:, lats, lats : 2 * lats, :], sem.at[fields + 1])
    )
    for n, (source, target) in enumerate(zip(small, small_out)):
        copies.append(pltpu.make_async_copy(source, target, sem.at[fields + 2 + n]))
    for copy in copies:
        copy.start()
    for copy in copies:
        copy.wait()
    odd = lax.rem(lax.axis_index("lat"), 2)
    for out, start in ((to_a, (1 - odd) * (lats - STEPS)), (to_b, odd * (lats - STEPS))):
        for lev in range(levs):
            for row in range(STEPS):
                out[lev, row] = own[lev, start + row].astype(jnp.bfloat16)
            out[lev, STEPS] = own[lev, lats].astype(jnp.bfloat16)


def chunks_of(blocks):
    sizes, left = [], blocks
    for share in SHARES:
        sizes.append(min(left, max(1, blocks * share // sum(SHARES))))
        left -= sizes[-1]
    sizes[-1] += left
    return [(sum(sizes[:n]), size) for n, size in enumerate(sizes) if size]


def obs_kernel(lats, chunks, owner, block_row, count, innov, oper, *refs):
    outs, (lhs, rhs, acc, sem) = refs[:-4], refs[-4:]
    obs_rows = innov.shape[1]
    blocks = oper.shape[0] // obs_rows
    rows = innov.shape[0] // blocks
    fields = 2 * lats
    levs = rows // fields
    def fetch_oper(first, length, n):
        some = pl.ds(pl.multiple_of(first, PIECE), pl.multiple_of(length, PIECE))
        return pltpu.make_async_copy(oper.at[some], rhs.at[some], sem.at[1, n])

    waits = {}
    for n, (at, size) in enumerate(chunks):
        some = pl.ds(at * rows, size * rows)
        copy = pltpu.make_async_copy(innov.at[some], lhs.at[some], sem.at[0, n])
        copy.start()
        total = 0
        for block in range(at, at + size):
            length = lax.shift_right_logical(count[block] + (PIECE - 1), BITS)
            length = lax.shift_left(length, BITS)
            fetch_oper(block * obs_rows, length, n).start()
            total = total + length
        waits[at] = (copy, fetch_oper(0, total, n))
    acc[...] = jnp.zeros_like(acc)
    place = lax.broadcasted_iota(jnp.int32, (obs_rows, rhs.shape[1]), 0)
    place = place.astype(jnp.float32).astype(jnp.bfloat16)
    for block in range(blocks):
        for copy in waits.get(block, ()):
            copy.wait()
        seen = place < count[block].astype(jnp.float32).astype(jnp.bfloat16)
        masked = rhs[block * obs_rows : (block + 1) * obs_rows, :]
        masked = jnp.where(seen, masked, jnp.zeros_like(masked))
        product = jnp.dot(
            lhs[block * rows : (block + 1) * rows, :], masked, preferred_element_type=jnp.float32
        )
        spot = owner[block] * lats + block_row[block]
        product = product.astype(jnp.bfloat16).astype(jnp.float32)
        for half in range(acc.shape[1]):
            part = product[:, half * LANES : (half + 1) * LANES]
            acc[spot, half] = acc[spot, half] + part

    def by_field(spot, lev):
        halves = [
            acc[spot, half, pl.ds(lev, fields, stride=levs), :] for half in range(acc.shape[1])
        ]
        return jnp.concatenate(halves, axis=1)

    if len(outs) == 2:
        mine = lax.axis_index("lon")
        for out, tile in zip(outs, (mine, 1 - mine)):
            for row in range(lats):
                for lev in range(levs):
                    out[lev, row] = by_field(tile * lats + row, lev).astype(out.dtype)
    else:
        (out,) = outs
        for tile in range(out.shape[0]):
            for row in range(lats):
                for lev in range(levs):
                    out[tile, lev, row] = by_field(tile * lats + row, lev)


def lat_kernel(own, from_a, from_b, obs, ext, to_a, to_b, edges, edges_a, edges_b):
    levs, lats = own.shape[0], own.shape[1] - 1
    place = lax.axis_index("lat")
    even = lax.rem(place, 2) == 0
    south_in = (place > 0).astype(jnp.float32)
    north_in = (place < lax.axis_size("lat") - 1).astype(jnp.float32)
    south_wind, own_wind, north_wind = lats + 2 * STEPS, lats + 2 * STEPS + 1, lats + 2 * STEPS + 2

    def fill(south, north):
        for lev in range(levs):
            for row in range(STEPS):
                ext[lev, row] = south[lev, row].astype(jnp.float32) * south_in
                ext[lev, STEPS + lats + row] = north[lev, row].astype(jnp.float32) * north_in
            ext[lev, south_wind] = south[lev, STEPS].astype(jnp.float32)
            ext[lev, north_wind] = north[lev, STEPS].astype(jnp.float32)

    @pl.when(even)
    def _():
        fill(from_b, from_a)

    @pl.when(jnp.logical_not(even))
    def _():
        fill(from_a, from_b)

    for lev in range(levs):
        for row in range(lats):
            ext[lev, STEPS + row] = own[lev, row]
        ext[lev, own_wind] = own[lev, lats]
    odd = lax.rem(lax.axis_index("lev"), 2)
    sub = lax.broadcasted_iota(jnp.int32, own.shape[2:], 0)
    outer = lax.rem(sub, lats) >= lats // 2
    for out, packed, down in ((to_a, edges_a, odd), (to_b, edges_b, 1 - odd)):
        tiles = []
        for d, first, rows in lev_rows(lats):
            lev = down * (d - 1) + (1 - down) * (levs - d)
            tiles += [ext[lev, STEPS + first + row] for row in range(rows)]
        for d in range(1, STEPS):
            lev = down * (d - 1) + (1 - down) * (levs - d)
            tiles.append(ext[lev, own_wind])
            tiles.append(jnp.where(outer, ext[lev, south_wind], ext[lev, north_wind]))
        for n, value in enumerate(tiles):
            out[n] = value.astype(jnp.bfloat16)
        pack(tiles, packed, 0)
    at = 0
    if edges.shape[0] > -(-levs * ext.shape[1] // PER_TILE):
        for lev in range(levs):
            for row in range(lats):
                for half in range(ext.shape[3] // LANES):
                    edges[at] = obs[lev, row, :, half * LANES : (half + 1) * LANES]
                    at += 1
    pack([ext[lev, n] for lev in range(levs) for n in range(ext.shape[1])], edges, at)


class Steps:
    def __init__(self, levs, lats, lev_tiles, level_total):
        self.levs, self.lats, self.level_total = levs, lats, level_total
        keys = [("ext", k, tile) for k in range(levs) for tile in range(lats + 2 * STEPS + 3)]
        keys += [("lev", side, tile) for side in range(2) for tile in range(lev_tiles)]
        self.order = {key: n for n, key in enumerate(keys)}
        self.starts, at = {}, 0
        for d, first, rows in lev_rows(lats):
            self.starts[d] = at - first
            at += rows
        self.winds_at = at
        self.cells = [
            (k, j) for k in range(-STEPS, levs + STEPS) for j in range(-STEPS, lats + STEPS)
        ]

    def distance(self, k, j):
        return max(-k, 0, k - self.levs + 1) + max(-j, 0, j - self.lats + 1)

    def spot(self, k, j):
        return (k + STEPS) * (self.lats + 2 * STEPS) + j + STEPS

    def side(self, k):
        return (0, -k) if k < 0 else (1, k - self.levs + 1)

    def source(self, k, j):
        if 0 <= k < self.levs:
            return ("ext", k, STEPS + j)
        side, d = self.side(k)
        return ("lev", side, self.starts[d] + j)

    def wind_source(self, k, j, which):
        tile = 0 if j < 0 else (1 if j < self.lats else 2)
        row = which * self.lats + j % self.lats
        if 0 <= k < self.levs:
            return ("ext", k, self.lats + 2 * STEPS + tile), row
        side, d = self.side(k)
        return ("lev", side, self.winds_at + 2 * (d - 1) + (0 if tile == 1 else 1)), row

    def run(self, diff, vert, shape, first_rows, wind, buffers, emit):
        levs, lats = self.levs, self.lats
        width = shape[1]
        lat_place, lev_place = lax.axis_index("lat"), lax.axis_index("lev")
        south_in = (lat_place > 0).astype(jnp.float32)
        north_in = (lat_place < lax.axis_size("lat") - 1).astype(jnp.float32)
        below_in = (lev_place > 0).astype(jnp.float32)
        above_in = (lev_place < lax.axis_size("lev") - 1).astype(jnp.float32)
        sub = lax.broadcasted_iota(jnp.int32, shape, 0)
        hd = jnp.zeros(shape, jnp.float32)
        for f in range(shape[0]):
            hd = jnp.where(sub == f, diff[f], hd)
        up, down = {}, {}
        for k in range(1 - STEPS, levs + STEPS - 1):
            level = lev_place * levs + k
            last = jnp.minimum(jnp.maximum(level, 0), self.level_total - 1)
            before = jnp.minimum(jnp.maximum(level - 1, 0), self.level_total - 1)
            up[k] = jnp.where(level < self.level_total - 1, vert[last], 0.0)
            down[k] = jnp.where(level >= 1, vert[before], 0.0)
        rows = first_rows
        for n in range(1, STEPS + 1):
            target = None if n == STEPS else buffers[(n - 1) % 2]
            for k, j in self.cells:
                if self.distance(k, j) > STEPS - n:
                    continue
                a = rows(k, j)
                u, w = wind(k, j, 0), wind(k, j, 1)
                new = a * (1.0 - up[k] - down[k] - u - w - 4.0 * hd)
                new = new + pltpu.roll((u + hd) * a, width - 1, 1) + hd * pltpu.roll(a, 1, 1)
                new = new + (wind(k, j + 1, 1) + hd) * rows(k, j + 1) + hd * rows(k, j - 1)
                new = new + up[k] * rows(k + 1, j) + down[k] * rows(k - 1, j)
                if k < 0:
                    new = new * below_in
                elif k >= levs:
                    new = new * above_in
                if j < 0:
                    new = new * south_in
                elif j >= lats:
                    new = new * north_in
                if target is None:
                    emit(k, j, new)
                else:
                    target[self.spot(k, j)] = new
            if target is not None:
                rows = functools.partial(lambda ref, k, j: ref[self.spot(k, j)], target)


EAST_END = LANES // 2
FIRST_AT = EAST_END + GROUP


def sides(low, high):
    place = lax.axis_index("lev")
    even = lax.rem(place, 2) == 0
    below_in = (place > 0).astype(jnp.float32)
    above_in = (place < lax.axis_size("lev") - 1).astype(jnp.float32)
    below, above = jnp.where(even, high, low), jnp.where(even, low, high)
    return below * below_in, above * above_in


def main_kernel(diff, vert, ext, from_a, from_b, result, edge_rows, lev, rows_a, rows_b):
    levs, lats = ext.shape[0], ext.shape[1] - 2 * STEPS - 3
    for tile in range(lev.shape[1]):
        low, high = from_a[tile].astype(jnp.float32), from_b[tile].astype(jnp.float32)
        lev[0, tile], lev[1, tile] = sides(low, high)
    steps = Steps(levs, lats, lev.shape[1], vert.shape[0])
    refs = {"ext": ext, "lev": lev}

    def first_rows(k, j):
        kind, i, tile = steps.source(k, j)
        return refs[kind][i, tile]

    def wind(k, j, which):
        (kind, i, tile), row = steps.wind_source(k, j, which)
        return refs[kind][i, tile, row : row + 1, :]

    def emit(k, j, new):
        result[k, j] = new

    steps.run(diff, vert, ext.shape[2:], first_rows, wind, (rows_a, rows_b), emit)
    lane = lax.broadcasted_iota(jnp.int32, edge_rows.shape[1:], 1)
    for n, (kind, i, tile) in enumerate(steps.order):
        first = pltpu.roll(refs[kind][i, tile, :, 0:LANES], FIRST_AT, 1)
        last = pltpu.roll(refs[kind][i, tile, :, -LANES:], EAST_END, 1)
        edge_rows[n] = jnp.where(lane < EAST_END, last, first)


def edge_kernel(levs, lats, lev_tiles, n_ways, diff, vert, main, own_rows, obs, *refs):
    halos, (out, edge_rows, rows_a, rows_b, result, sem) = refs[: 3 * n_ways], refs[3 * n_ways :]
    fields, lons = main.shape[2:]
    parts = lons // LANES
    steps = Steps(levs, lats, lev_tiles, vert.shape[0])
    lane = lax.broadcasted_iota(jnp.int32, (fields, LANES), 1)
    in_halo = (lane >= EAST_END) & (lane < FIRST_AT)
    ext_rows = len(steps.order) - 2 * lev_tiles
    obs_at = levs * lats * parts if n_ways == 1 else 0

    def packed(which, n):
        tiles = [halos[3 * way + which][n].astype(jnp.float32) for way in range(n_ways)]
        return jnp.where(lane % GROUP < GROUP // 2, tiles[-1], tiles[0])

    def unpack(tile, at, count):
        for k in range(count):
            halo = pltpu.roll(tile, (EAST_END - GROUP * k) % LANES, 1)
            edge_rows[at + k] = jnp.where(in_halo, halo, own_rows[at + k])

    for at in range(0, ext_rows, PER_TILE):
        unpack(packed(0, obs_at + at // PER_TILE), at, min(PER_TILE, ext_rows - at))
    for at in range(0, lev_tiles, PER_TILE):
        both = sides(packed(1, at // PER_TILE), packed(2, at // PER_TILE))
        for side, tile in enumerate(both):
            start = ext_rows + side * lev_tiles + at
            unpack(tile, start, min(PER_TILE, lev_tiles - at))

    def first_rows(k, j):
        return edge_rows[steps.order[steps.source(k, j)]]

    def wind(k, j, which):
        key, row = steps.wind_source(k, j, which)
        return edge_rows[steps.order[key], row : row + 1, :]

    def total(k, j, part):
        value = obs[k, j, :, part * LANES : (part + 1) * LANES]
        if n_ways == 1:
            value = value + halos[0][(k * lats + j) * parts + part].astype(jnp.float32)
        return value

    def emit(k, j, new):
        first = pltpu.roll(new, LANES - FIRST_AT, 1)
        last = pltpu.roll(new, LANES - EAST_END, 1)
        for part in range(parts):
            value = main[k, j, :, part * LANES : (part + 1) * LANES]
            if part == 0:
                value = jnp.where(lane < STEPS, first, value)
            if part == parts - 1:
                value = jnp.where(lane >= LANES - STEPS, last, value)
            result[k, j, :, part * LANES : (part + 1) * LANES] = value + total(k, j, part)

    steps.run(diff, vert, (fields, LANES), first_rows, wind, (rows_a, rows_b), emit)
    copies = [
        pltpu.make_async_copy(result.at[:, :, f, :], out.at[f], sem.at[f]) for f in range(fields)
    ]
    for copy in copies:
        copy.start()
    for copy in copies:
        copy.wait()


def on_device(
    adjoint_in,
    courant_lon,
    courant_lat,
    horiz_diff,
    vert_diff,
    innovations,
    obs_operator,
    owner_tile,
    block_row,
    obs_count,
):
    fields, levs, lats, lons = adjoint_in.shape
    blocks, _, _, obs_rows = innovations.shape
    n_lon, n_lat, n_lev = (lax.axis_size(axis) for axis in ("lon", "lat", "lev"))
    f32, bf16 = jnp.float32, jnp.bfloat16
    assert lats >= STEPS and levs >= STEPS and lons % LANES == 0 and fields == 2 * lats

    tile = (fields, lons)
    smalls = (owner_tile[:, 0], block_row, obs_count)
    inputs = (adjoint_in, courant_lon, courant_lat) + smalls
    own, to_lat_a, to_lat_b, *smalls = pl.pallas_call(
        load_kernel,
        out_shape=(
            jax.ShapeDtypeStruct((levs, lats + 1) + tile, f32),
            jax.ShapeDtypeStruct((levs, STEPS + 1) + tile, bf16),
            jax.ShapeDtypeStruct((levs, STEPS + 1) + tile, bf16),
        )
        + tuple(jax.ShapeDtypeStruct(x.shape, x.dtype) for x in smalls),
        in_specs=[HBM] * 6,
        out_specs=(VMEM,) * 6,
        scratch_shapes=[pltpu.SemaphoreType.DMA((fields + 5,))],
        cost_estimate=cost(1, 64 << 20),
        compiler_params=PARAMS,
        name="load",
    )(*(pltpu.with_memory_space_constraint(x, pltpu.HBM) for x in inputs))
    sizes = (n_lon, n_lat, n_lev)
    from_lat_a = send(to_lat_a, pair_up(sizes, 1, 0))
    from_lat_b = send(to_lat_b, pair_up(sizes, 1, 1))

    chunks = chunks_of(blocks)
    rows = fields * levs
    targets = n_lon * lats
    if n_lon == 2:
        obs_out = (
            jax.ShapeDtypeStruct((levs, lats) + tile, f32),
            jax.ShapeDtypeStruct((levs, lats) + tile, bf16),
        )
    else:
        obs_out = (jax.ShapeDtypeStruct((n_lon, levs, lats) + tile, f32),)
    obs = pl.pallas_call(
        functools.partial(obs_kernel, lats, chunks),
        out_shape=obs_out,
        in_specs=[SMEM] * 3 + [HBM] * 2,
        out_specs=(VMEM,) * len(obs_out),
        scratch_shapes=[
            pltpu.VMEM((blocks * rows, obs_rows), bf16),
            pltpu.VMEM((blocks * obs_rows, lons), bf16),
            pltpu.VMEM((targets, lons // LANES, rows, LANES), f32),
            pltpu.SemaphoreType.DMA((2, len(chunks))),
        ],
        cost_estimate=cost(2 * blocks * rows * obs_rows * lons, 12 << 20),
        compiler_params=PARAMS,
        name="obs",
    )(
        *smalls,
        pltpu.with_memory_space_constraint(
            innovations.reshape(blocks * rows, obs_rows), pltpu.HBM
        ),
        pltpu.with_memory_space_constraint(
            obs_operator.reshape(blocks * obs_rows, lons), pltpu.HBM
        ),
    )

    lev_tiles = sum(rows for _, _, rows in lev_rows(lats)) + 2 * (STEPS - 1)
    ext_tiles = lats + 2 * STEPS + 3
    ext_packed, lev_packed = -(-levs * ext_tiles // PER_TILE), -(-lev_tiles // PER_TILE)
    obs_tiles = levs * lats * (lons // LANES) if n_lon == 2 else 0
    lane_tile = (fields, LANES)
    ext, to_lev_a, to_lev_b, edges, edges_a, edges_b = pl.pallas_call(
        lat_kernel,
        out_shape=(
            jax.ShapeDtypeStruct((levs, ext_tiles) + tile, f32),
            jax.ShapeDtypeStruct((lev_tiles,) + tile, bf16),
            jax.ShapeDtypeStruct((lev_tiles,) + tile, bf16),
            jax.ShapeDtypeStruct((obs_tiles + ext_packed,) + lane_tile, bf16),
            jax.ShapeDtypeStruct((lev_packed,) + lane_tile, bf16),
            jax.ShapeDtypeStruct((lev_packed,) + lane_tile, bf16),
        ),
        in_specs=[VMEM] * 4,
        out_specs=(VMEM,) * 6,
        cost_estimate=cost(1, 1 << 20),
        compiler_params=PARAMS,
        name="extend_lat",
    )(own, from_lat_a, from_lat_b, obs[-1])
    from_lev_b = send(to_lev_b, pair_up(sizes, 2, 1))
    from_lev_a = send(to_lev_a, pair_up(sizes, 2, 0))
    ways = (1,) if n_lon == 2 else (1, -1)
    halos = []
    for way in ways:
        halos.append(send(edges, pair_up(sizes, 0, 0, way)))
        halos.append(send(edges_a, pair_up(sizes, 2, 0, way)))
        halos.append(send(edges_b, pair_up(sizes, 2, 1, way)))
    if n_lon == 2:
        obs_own = obs[0]
    else:
        flat = obs[0].reshape(-1, lons)
        obs_own = lax.psum_scatter(flat, "lon", scatter_dimension=0, tiled=True)
        obs_own = obs_own.reshape((levs, lats) + tile)

    grid_rows = (levs + 2 * STEPS) * (lats + 2 * STEPS)
    edge_shape = (levs * ext_tiles + 2 * lev_tiles,) + lane_tile
    main, edge_rows = pl.pallas_call(
        main_kernel,
        out_shape=(
            jax.ShapeDtypeStruct((levs, lats) + tile, f32),
            jax.ShapeDtypeStruct(edge_shape, f32),
        ),
        in_specs=[SMEM] * 2 + [VMEM] * 3,
        out_specs=(VMEM,) * 2,
        scratch_shapes=[pltpu.VMEM((2, lev_tiles) + tile, f32)]
        + [pltpu.VMEM((grid_rows,) + tile, f32)] * 2,
        cost_estimate=cost(1, 8 << 20),
        compiler_params=PARAMS,
        name="sub_steps",
    )(horiz_diff, vert_diff, ext, from_lev_a, from_lev_b)
    return pl.pallas_call(
        functools.partial(edge_kernel, levs, lats, lev_tiles, len(ways)),
        out_shape=jax.ShapeDtypeStruct(adjoint_in.shape, f32),
        in_specs=[SMEM] * 2 + [VMEM] * (3 + len(halos)),
        out_specs=ANY,
        scratch_shapes=[
            pltpu.VMEM(edge_shape, f32),
            pltpu.VMEM((grid_rows, fields, LANES), f32),
            pltpu.VMEM((grid_rows, fields, LANES), f32),
            pltpu.VMEM((levs, lats) + tile, f32),
            pltpu.SemaphoreType.DMA((fields,)),
        ],
        cost_estimate=cost(1, 1 << 20),
        compiler_params=PARAMS,
        name="edges",
    )(horiz_diff, vert_diff, main, edge_rows, obs_own, *halos)


def solution(mesh):
    in_specs = (
        P(None, "lev", "lat", "lon"),
        P("lev", "lat", "lon"),
        P("lev", "lat", "lon"),
        P(),
        P(),
        P(("lon", "lat"), None, "lev", None),
        P(("lon", "lat"), None, None),
        P(("lon", "lat"), None),
        P(("lon", "lat")),
        P(("lon", "lat")),
    )
    out_specs = P(None, "lev", "lat", "lon")
    return jax.shard_map(
        on_device, mesh=mesh, in_specs=in_specs, out_specs=out_specs, check_vma=False
    )
```

```python
import functools

import jax
import jax.numpy as jnp
from jax import lax
from jax.experimental import pallas as pl
from jax.experimental.pallas import tpu as pltpu
from jax.sharding import PartitionSpec as P


STEPS = 3
LANES = 128
GROUP = 16
PER_TILE = LANES // GROUP
BITS = 4
PIECE = 1 << BITS
SHARES = (1,) * 3
VMEM = pl.BlockSpec(memory_space=pltpu.VMEM)
SMEM = pl.BlockSpec(memory_space=pltpu.SMEM)
ANY = pl.BlockSpec(memory_space=pl.ANY)
HBM = pl.BlockSpec(memory_space=pltpu.HBM)


PARAMS = pltpu.CompilerParams(vmem_limit_bytes=12 << 20)


def cost(flops, nbytes):
    return pl.CostEstimate(flops=flops, bytes_accessed=nbytes, transcendentals=0)


def pair_up(sizes, axis, phase, shift=0):
    n_lon, n_lat, n_lev = sizes
    pairs = []
    for lon in range(n_lon):
        for lat in range(n_lat):
            for lev in range(n_lev):
                to = [(lon + shift) % n_lon, lat, lev]
                if axis:
                    mate = to[axis] + (1 if to[axis] % 2 == phase else -1)
                    if 0 <= mate < sizes[axis]:
                        to[axis] = mate
                    elif shift % n_lon == 0:
                        to[3 - axis] ^= 1
                        if to[3 - axis] >= sizes[3 - axis]:
                            continue
                ends = [(p * n_lat + q) * n_lev + r for p, q, r in ((lon, lat, lev), to)]
                pairs.append(tuple(ends))
    return pairs


def send(x, pairs):
    return lax.ppermute(x, ("lon", "lat", "lev"), pairs)


def pack(tiles, out, at):
    total = None
    for n, value in enumerate(tiles):
        k = n % PER_TILE
        lane = lax.broadcasted_iota(jnp.int32, (value.shape[0], LANES), 1)
        value = jnp.where(lane < LANES // 2, value[:, 0:LANES], value[:, -LANES:])
        if k:
            value = pltpu.roll(value, GROUP * k, 1)
            value = jnp.where((lane + STEPS) % LANES // GROUP == k, value, total)
        total = value
        if k == PER_TILE - 1 or n == len(tiles) - 1:
            total = jnp.where(lane % GROUP < GROUP // 2, total, pltpu.roll(total, GROUP, 1))
            out[at + n // PER_TILE] = total.astype(out.dtype)


def lev_rows(lat_cells):
    return [(d, -(STEPS - d), lat_cells + 2 * (STEPS - d)) for d in range(1, STEPS + 1)]


def load_kernel(adj, wind_u, wind_w, *refs):
    small, (own, to_a, to_b), small_out, sem = refs[:3], refs[3:6], refs[6:9], refs[9]
    fields, levs, lats = adj.shape[:3]
    copies = [
        pltpu.make_async_copy(adj.at[f], own.at[:, 0:lats, f, :], sem.at[f]) for f in range(fields)
    ]
    copies.append(pltpu.make_async_copy(wind_u, own.at[:, lats, 0:lats, :], sem.at[fields]))
    copies.append(
        pltpu.make_async_copy(wind_w, own.at[:, lats, lats : 2 * lats, :], sem.at[fields + 1])
    )
    for n, (source, target) in enumerate(zip(small, small_out)):
        copies.append(pltpu.make_async_copy(source, target, sem.at[fields + 2 + n]))
    for copy in copies:
        copy.start()
    for copy in copies:
        copy.wait()
    odd = lax.rem(lax.axis_index("lat"), 2)
    for out, start in ((to_a, (1 - odd) * (lats - STEPS)), (to_b, odd * (lats - STEPS))):
        for lev in range(levs):
            for row in range(STEPS):
                out[lev, row] = own[lev, start + row].astype(jnp.bfloat16)
            out[lev, STEPS] = own[lev, lats].astype(jnp.bfloat16)


def chunks_of(blocks):
    sizes, left = [], blocks
    for share in SHARES:
        sizes.append(min(left, max(1, blocks * share // sum(SHARES))))
        left -= sizes[-1]
    sizes[-1] += left
    return [(sum(sizes[:n]), size) for n, size in enumerate(sizes) if size]


def obs_kernel(lats, chunks, owner, block_row, count, innov, oper, *refs):
    outs, (lhs, rhs, acc, sem) = refs[:-4], refs[-4:]
    obs_rows = innov.shape[1]
    blocks = oper.shape[0] // obs_rows
    rows = innov.shape[0] // blocks
    fields = 2 * lats
    levs = rows // fields

    def fetch_oper(first, length, n):
        some = pl.ds(pl.multiple_of(first, PIECE), pl.multiple_of(length, PIECE))
        return pltpu.make_async_copy(oper.at[some], rhs.at[some], sem.at[1, n])

    waits = {}
    for n, (at, size) in enumerate(chunks):
        some = pl.ds(at * rows, size * rows)
        copy = pltpu.make_async_copy(innov.at[some], lhs.at[some], sem.at[0, n])
        copy.start()
        total = 0
        for block in range(at, at + size):
            length = lax.shift_right_logical(count[block] + (PIECE - 1), BITS)
            length = lax.shift_left(length, BITS)
            fetch_oper(block * obs_rows, length, n).start()
            total = total + length
        waits[at] = (copy, fetch_oper(0, total, n))
    acc[...] = jnp.zeros_like(acc)
    place = lax.broadcasted_iota(jnp.int32, (obs_rows, rhs.shape[1]), 0)
    place = place.astype(jnp.float32).astype(jnp.bfloat16)
    for block in range(blocks):
        for copy in waits.get(block, ()):
            copy.wait()
        seen = place < count[block].astype(jnp.float32).astype(jnp.bfloat16)
        masked = rhs[block * obs_rows : (block + 1) * obs_rows, :]
        masked = jnp.where(seen, masked, jnp.zeros_like(masked))
        product = jnp.dot(
            lhs[block * rows : (block + 1) * rows, :], masked, preferred_element_type=jnp.float32
        )
        spot = owner[block] * lats + block_row[block]
        product = product.astype(jnp.bfloat16).astype(jnp.float32)
        for half in range(acc.shape[1]):
            part = product[:, half * LANES : (half + 1) * LANES]
            acc[spot, half] = acc[spot, half] + part

    def by_field(spot, lev):
        halves = [
            acc[spot, half, pl.ds(lev, fields, stride=levs), :] for half in range(acc.shape[1])
        ]
        return jnp.concatenate(halves, axis=1)

    if len(outs) == 2:
        mine = lax.axis_index("lon")
        for out, tile in zip(outs, (mine, 1 - mine)):
            for row in range(lats):
                for lev in range(levs):
                    out[lev, row] = by_field(tile * lats + row, lev).astype(out.dtype)
    else:
        (out,) = outs
        for tile in range(out.shape[0]):
            for row in range(lats):
                for lev in range(levs):
                    out[tile, lev, row] = by_field(tile * lats + row, lev)


def lat_kernel(own, from_a, from_b, obs, ext, to_a, to_b, edges, edges_a, edges_b):
    levs, lats = own.shape[0], own.shape[1] - 1
    place = lax.axis_index("lat")
    even = lax.rem(place, 2) == 0
    south_in = (place > 0).astype(jnp.float32)
    north_in = (place < lax.axis_size("lat") - 1).astype(jnp.float32)
    south_wind, own_wind, north_wind = lats + 2 * STEPS, lats + 2 * STEPS + 1, lats + 2 * STEPS + 2

    def fill(south, north):
        for lev in range(levs):
            for row in range(STEPS):
                ext[lev, row] = south[lev, row].astype(jnp.float32) * south_in
                ext[lev, STEPS + lats + row] = north[lev, row].astype(jnp.float32) * north_in
            ext[lev, south_wind] = south[lev, STEPS].astype(jnp.float32)
            ext[lev, north_wind] = north[lev, STEPS].astype(jnp.float32)

    @pl.when(even)
    def _():
        fill(from_b, from_a)

    @pl.when(jnp.logical_not(even))
    def _():
        fill(from_a, from_b)

    for lev in range(levs):
        for row in range(lats):
            ext[lev, STEPS + row] = own[lev, row]
        ext[lev, own_wind] = own[lev, lats]
    odd = lax.rem(lax.axis_index("lev"), 2)
    sub = lax.broadcasted_iota(jnp.int32, own.shape[2:], 0)
    outer = lax.rem(sub, lats) >= lats // 2
    for out, packed, down in ((to_a, edges_a, odd), (to_b, edges_b, 1 - odd)):
        tiles = []
        for d, first, rows in lev_rows(lats):
            lev = down * (d - 1) + (1 - down) * (levs - d)
            tiles += [ext[lev, STEPS + first + row] for row in range(rows)]
        for d in range(1, STEPS):
            lev = down * (d - 1) + (1 - down) * (levs - d)
            tiles.append(ext[lev, own_wind])
            tiles.append(jnp.where(outer, ext[lev, south_wind], ext[lev, north_wind]))
        for n, value in enumerate(tiles):
            out[n] = value.astype(jnp.bfloat16)
        pack(tiles, packed, 0)
    at = 0
    if edges.shape[0] > -(-levs * ext.shape[1] // PER_TILE):
        for lev in range(levs):
            for row in range(lats):
                for half in range(ext.shape[3] // LANES):
                    edges[at] = obs[lev, row, :, half * LANES : (half + 1) * LANES]
                    at += 1
    pack([ext[lev, n] for lev in range(levs) for n in range(ext.shape[1])], edges, at)


class Steps:
    def __init__(self, levs, lats, lev_tiles, level_total):
        self.levs, self.lats, self.level_total = levs, lats, level_total
        keys = [("ext", k, tile) for k in range(levs) for tile in range(lats + 2 * STEPS + 3)]
        keys += [("lev", side, tile) for side in range(2) for tile in range(lev_tiles)]
        self.order = {key: n for n, key in enumerate(keys)}
        self.starts, at = {}, 0
        for d, first, rows in lev_rows(lats):
            self.starts[d] = at - first
            at += rows
        self.winds_at = at
        self.cells = [
            (k, j) for k in range(-STEPS, levs + STEPS) for j in range(-STEPS, lats + STEPS)
        ]

    def distance(self, k, j):
        return max(-k, 0, k - self.levs + 1) + max(-j, 0, j - self.lats + 1)

    def spot(self, k, j):
        return (k + STEPS) * (self.lats + 2 * STEPS) + j + STEPS

    def side(self, k):
        return (0, -k) if k < 0 else (1, k - self.levs + 1)

    def source(self, k, j):
        if 0 <= k < self.levs:
            return ("ext", k, STEPS + j)
        side, d = self.side(k)
        return ("lev", side, self.starts[d] + j)

    def wind_source(self, k, j, which):
        tile = 0 if j < 0 else (1 if j < self.lats else 2)
        row = which * self.lats + j % self.lats
        if 0 <= k < self.levs:
            return ("ext", k, self.lats + 2 * STEPS + tile), row
        side, d = self.side(k)
        return ("lev", side, self.winds_at + 2 * (d - 1) + (0 if tile == 1 else 1)), row

    def run(self, diff, vert, shape, first_rows, wind, buffers, emit):
        levs, lats = self.levs, self.lats
        width = shape[1]
        lat_place, lev_place = lax.axis_index("lat"), lax.axis_index("lev")
        south_in = (lat_place > 0).astype(jnp.float32)
        north_in = (lat_place < lax.axis_size("lat") - 1).astype(jnp.float32)
        below_in = (lev_place > 0).astype(jnp.float32)
        above_in = (lev_place < lax.axis_size("lev") - 1).astype(jnp.float32)
        sub = lax.broadcasted_iota(jnp.int32, shape, 0)
        hd = jnp.zeros(shape, jnp.float32)
        for f in range(shape[0]):
            hd = jnp.where(sub == f, diff[f], hd)
        up, down = {}, {}
        for k in range(1 - STEPS, levs + STEPS - 1):
            level = lev_place * levs + k
            last = jnp.minimum(jnp.maximum(level, 0), self.level_total - 1)
            before = jnp.minimum(jnp.maximum(level - 1, 0), self.level_total - 1)
            up[k] = jnp.where(level < self.level_total - 1, vert[last], 0.0)
            down[k] = jnp.where(level >= 1, vert[before], 0.0)
        rows = first_rows
        for n in range(1, STEPS + 1):
            target = None if n == STEPS else buffers[(n - 1) % 2]
            for k, j in self.cells:
                if self.distance(k, j) > STEPS - n:
                    continue
                a = rows(k, j)
                u, w = wind(k, j, 0), wind(k, j, 1)
                new = a * (1.0 - up[k] - down[k] - u - w - 4.0 * hd)
                new = new + pltpu.roll((u + hd) * a, width - 1, 1) + hd * pltpu.roll(a, 1, 1)
                new = new + (wind(k, j + 1, 1) + hd) * rows(k, j + 1) + hd * rows(k, j - 1)
                new = new + up[k] * rows(k + 1, j) + down[k] * rows(k - 1, j)
                if k < 0:
                    new = new * below_in
                elif k >= levs:
                    new = new * above_in
                if j < 0:
                    new = new * south_in
                elif j >= lats:
                    new = new * north_in
                if target is None:
                    emit(k, j, new)
                else:
                    target[self.spot(k, j)] = new
            if target is not None:
                rows = functools.partial(lambda ref, k, j: ref[self.spot(k, j)], target)


EAST_END = LANES // 2
FIRST_AT = EAST_END + GROUP


def sides(low, high):
    place = lax.axis_index("lev")
    even = lax.rem(place, 2) == 0
    below_in = (place > 0).astype(jnp.float32)
    above_in = (place < lax.axis_size("lev") - 1).astype(jnp.float32)
    below, above = jnp.where(even, high, low), jnp.where(even, low, high)
    return below * below_in, above * above_in


def main_kernel(diff, vert, ext, from_a, from_b, result, edge_rows, lev, rows_a, rows_b):
    levs, lats = ext.shape[0], ext.shape[1] - 2 * STEPS - 3
    for tile in range(lev.shape[1]):
        low, high = from_a[tile].astype(jnp.float32), from_b[tile].astype(jnp.float32)
        lev[0, tile], lev[1, tile] = sides(low, high)
    steps = Steps(levs, lats, lev.shape[1], vert.shape[0])
    refs = {"ext": ext, "lev": lev}

    def first_rows(k, j):
        kind, i, tile = steps.source(k, j)
        return refs[kind][i, tile]

    def wind(k, j, which):
        (kind, i, tile), row = steps.wind_source(k, j, which)
        return refs[kind][i, tile, row : row + 1, :]

    def emit(k, j, new):
        result[k, j] = new

    steps.run(diff, vert, ext.shape[2:], first_rows, wind, (rows_a, rows_b), emit)
    lane = lax.broadcasted_iota(jnp.int32, edge_rows.shape[1:], 1)
    for n, (kind, i, tile) in enumerate(steps.order):
        first = pltpu.roll(refs[kind][i, tile, :, 0:LANES], FIRST_AT, 1)
        last = pltpu.roll(refs[kind][i, tile, :, -LANES:], EAST_END, 1)
        edge_rows[n] = jnp.where(lane < EAST_END, last, first)


def edge_kernel(levs, lats, lev_tiles, n_ways, diff, vert, main, own_rows, obs, *refs):
    halos, (out, edge_rows, rows_a, rows_b, result, sem) = refs[: 3 * n_ways], refs[3 * n_ways :]
    fields, lons = main.shape[2:]
    parts = lons // LANES
    steps = Steps(levs, lats, lev_tiles, vert.shape[0])
    lane = lax.broadcasted_iota(jnp.int32, (fields, LANES), 1)
    in_halo = (lane >= EAST_END) & (lane < FIRST_AT)
    ext_rows = len(steps.order) - 2 * lev_tiles
    obs_at = levs * lats * parts if n_ways == 1 else 0

    def packed(which, n):
        tiles = [halos[3 * way + which][n].astype(jnp.float32) for way in range(n_ways)]
        return jnp.where(lane % GROUP < GROUP // 2, tiles[-1], tiles[0])

    def unpack(tile, at, count):
        for k in range(count):
            halo = pltpu.roll(tile, (EAST_END - GROUP * k) % LANES, 1)
            edge_rows[at + k] = jnp.where(in_halo, halo, own_rows[at + k])

    for at in range(0, ext_rows, PER_TILE):
        unpack(packed(0, obs_at + at // PER_TILE), at, min(PER_TILE, ext_rows - at))
    for at in range(0, lev_tiles, PER_TILE):
        both = sides(packed(1, at // PER_TILE), packed(2, at // PER_TILE))
        for side, tile in enumerate(both):
            start = ext_rows + side * lev_tiles + at
            unpack(tile, start, min(PER_TILE, lev_tiles - at))

    def first_rows(k, j):
        return edge_rows[steps.order[steps.source(k, j)]]

    def wind(k, j, which):
        key, row = steps.wind_source(k, j, which)
        return edge_rows[steps.order[key], row : row + 1, :]

    def total(k, j, part):
        value = obs[k, j, :, part * LANES : (part + 1) * LANES]
        if n_ways == 1:
            value = value + halos[0][(k * lats + j) * parts + part].astype(jnp.float32)
        return value

    def emit(k, j, new):
        first = pltpu.roll(new, LANES - FIRST_AT, 1)
        last = pltpu.roll(new, LANES - EAST_END, 1)
        for part in range(parts):
            value = main[k, j, :, part * LANES : (part + 1) * LANES]
            if part == 0:
                value = jnp.where(lane < STEPS, first, value)
            if part == parts - 1:
                value = jnp.where(lane >= LANES - STEPS, last, value)
            result[part, pl.ds(k * lats + j, fields, stride=levs * lats), :] = value + total(
                k, j, part
            )

    steps.run(diff, vert, (fields, LANES), first_rows, wind, (rows_a, rows_b), emit)
    copies = []
    for part in range(parts):
        some = pl.ds(part * LANES, LANES)
        source = result.at[part].reshape(fields, levs, lats, LANES)
        copies.append(
            pltpu.make_async_copy(source, out.at[:, :, :, some], sem.at[part])
        )
        copies[-1].start()
    for copy in copies:
        copy.wait()


def on_device(
    adjoint_in,
    courant_lon,
    courant_lat,
    horiz_diff,
    vert_diff,
    innovations,
    obs_operator,
    owner_tile,
    block_row,
    obs_count,
):
    fields, levs, lats, lons = adjoint_in.shape
    blocks, _, _, obs_rows = innovations.shape
    n_lon, n_lat, n_lev = (lax.axis_size(axis) for axis in ("lon", "lat", "lev"))
    f32, bf16 = jnp.float32, jnp.bfloat16
    assert lats >= STEPS and levs >= STEPS and lons % LANES == 0 and fields == 2 * lats

    tile = (fields, lons)
    smalls = (owner_tile[:, 0], block_row, obs_count)
    inputs = (adjoint_in, courant_lon, courant_lat) + smalls
    own, to_lat_a, to_lat_b, *smalls = pl.pallas_call(
        load_kernel,
        out_shape=(
            jax.ShapeDtypeStruct((levs, lats + 1) + tile, f32),
            jax.ShapeDtypeStruct((levs, STEPS + 1) + tile, bf16),
            jax.ShapeDtypeStruct((levs, STEPS + 1) + tile, bf16),
        )
        + tuple(jax.ShapeDtypeStruct(x.shape, x.dtype) for x in smalls),
        in_specs=[HBM] * 6,
        out_specs=(VMEM,) * 6,
        scratch_shapes=[pltpu.SemaphoreType.DMA((fields + 5,))],
        cost_estimate=cost(1, 64 << 20),
        compiler_params=PARAMS,
        name="load",
    )(*(pltpu.with_memory_space_constraint(x, pltpu.HBM) for x in inputs))
    sizes = (n_lon, n_lat, n_lev)
    from_lat_a = send(to_lat_a, pair_up(sizes, 1, 0))
    from_lat_b = send(to_lat_b, pair_up(sizes, 1, 1))

    chunks = chunks_of(blocks)
    rows = fields * levs
    targets = n_lon * lats
    if n_lon == 2:
        obs_out = (
            jax.ShapeDtypeStruct((levs, lats) + tile, f32),
            jax.ShapeDtypeStruct((levs, lats) + tile, bf16),
        )
    else:
        obs_out = (jax.ShapeDtypeStruct((n_lon, levs, lats) + tile, f32),)
    obs = pl.pallas_call(
        functools.partial(obs_kernel, lats, chunks),
        out_shape=obs_out,
        in_specs=[SMEM] * 3 + [HBM] * 2,
        out_specs=(VMEM,) * len(obs_out),
        scratch_shapes=[
            pltpu.VMEM((blocks * rows, obs_rows), bf16),
            pltpu.VMEM((blocks * obs_rows, lons), bf16),
            pltpu.VMEM((targets, lons // LANES, rows, LANES), f32),
            pltpu.SemaphoreType.DMA((2, len(chunks))),
        ],
        cost_estimate=cost(2 * blocks * rows * obs_rows * lons, 12 << 20),
        compiler_params=PARAMS,
        name="obs",
    )(
        *smalls,
        pltpu.with_memory_space_constraint(
            innovations.reshape(blocks * rows, obs_rows), pltpu.HBM
        ),
        pltpu.with_memory_space_constraint(
            obs_operator.reshape(blocks * obs_rows, lons), pltpu.HBM
        ),
    )

    lev_tiles = sum(rows for _, _, rows in lev_rows(lats)) + 2 * (STEPS - 1)
    ext_tiles = lats + 2 * STEPS + 3
    ext_packed, lev_packed = -(-levs * ext_tiles // PER_TILE), -(-lev_tiles // PER_TILE)
    obs_tiles = levs * lats * (lons // LANES) if n_lon == 2 else 0
    lane_tile = (fields, LANES)
    ext, to_lev_a, to_lev_b, edges, edges_a, edges_b = pl.pallas_call(
        lat_kernel,
        out_shape=(
            jax.ShapeDtypeStruct((levs, ext_tiles) + tile, f32),
            jax.ShapeDtypeStruct((lev_tiles,) + tile, bf16),
            jax.ShapeDtypeStruct((lev_tiles,) + tile, bf16),
            jax.ShapeDtypeStruct((obs_tiles + ext_packed,) + lane_tile, bf16),
            jax.ShapeDtypeStruct((lev_packed,) + lane_tile, bf16),
            jax.ShapeDtypeStruct((lev_packed,) + lane_tile, bf16),
        ),
        in_specs=[VMEM] * 4,
        out_specs=(VMEM,) * 6,
        cost_estimate=cost(1, 1 << 20),
        compiler_params=PARAMS,
        name="extend_lat",
    )(own, from_lat_a, from_lat_b, obs[-1])
    from_lev_b = send(to_lev_b, pair_up(sizes, 2, 1))
    from_lev_a = send(to_lev_a, pair_up(sizes, 2, 0))
    ways = (1,) if n_lon == 2 else (1, -1)
    halos = []
    for way in ways:
        halos.append(send(edges, pair_up(sizes, 0, 0, way)))
        halos.append(send(edges_a, pair_up(sizes, 2, 0, way)))
        halos.append(send(edges_b, pair_up(sizes, 2, 1, way)))
    if n_lon == 2:
        obs_own = obs[0]
    else:
        flat = obs[0].reshape(-1, lons)
        obs_own = lax.psum_scatter(flat, "lon", scatter_dimension=0, tiled=True)
        obs_own = obs_own.reshape((levs, lats) + tile)

    grid_rows = (levs + 2 * STEPS) * (lats + 2 * STEPS)
    edge_shape = (levs * ext_tiles + 2 * lev_tiles,) + lane_tile
    main, edge_rows = pl.pallas_call(
        main_kernel,
        out_shape=(
            jax.ShapeDtypeStruct((levs, lats) + tile, f32),
            jax.ShapeDtypeStruct(edge_shape, f32),
        ),
        in_specs=[SMEM] * 2 + [VMEM] * 3,
        out_specs=(VMEM,) * 2,
        scratch_shapes=[pltpu.VMEM((2, lev_tiles) + tile, f32)]
        + [pltpu.VMEM((grid_rows,) + tile, f32)] * 2,
        cost_estimate=cost(1, 8 << 20),
        compiler_params=PARAMS,
        name="sub_steps",
    )(horiz_diff, vert_diff, ext, from_lev_a, from_lev_b)
    return pl.pallas_call(
        functools.partial(edge_kernel, levs, lats, lev_tiles, len(ways)),
        out_shape=jax.ShapeDtypeStruct(adjoint_in.shape, f32),
        in_specs=[SMEM] * 2 + [VMEM] * (3 + len(halos)),
        out_specs=ANY,
        scratch_shapes=[
            pltpu.VMEM(edge_shape, f32),
            pltpu.VMEM((grid_rows, fields, LANES), f32),
            pltpu.VMEM((grid_rows, fields, LANES), f32),
            pltpu.VMEM((lons // LANES, fields * levs * lats, LANES), f32),
            pltpu.SemaphoreType.DMA((fields,)),
        ],
        cost_estimate=cost(1, 1 << 20),
        compiler_params=PARAMS,
        name="edges",
    )(horiz_diff, vert_diff, main, edge_rows, obs_own, *halos)


def solution(mesh):
    in_specs = (
        P(None, "lev", "lat", "lon"),
        P("lev", "lat", "lon"),
        P("lev", "lat", "lon"),
        P(),
        P(),
        P(("lon", "lat"), None, "lev", None),
        P(("lon", "lat"), None, None),
        P(("lon", "lat"), None),
        P(("lon", "lat")),
        P(("lon", "lat")),
    )
    out_specs = P(None, "lev", "lat", "lon")

    return jax.shard_map(
        on_device, mesh=mesh, in_specs=in_specs, out_specs=out_specs, check_vma=False
    )
```
